32 devices in a mesh: branch: 2 (over core), dap: 4 (over z), rep: 4 (over y, x).
Axes of the slice: x: 2, y: 2, z: 4, core: 2. Of those that a mesh axis runs over, the one named last changes fastest.
Arguments:
- homolog_stack: bfloat16 [512, 32, 256], P(('rep', 'branch', 'dap')), parts along dimension 0, may hold values from -6 to 6
- homolog_validity_flags: int32 [512], P(('rep', 'branch', 'dap')), parts along dimension 0, may hold values 0 or 1
- amino_validity_flags: int32 [128], P('rep'), parts along dimension 0, may hold values from 0 to 1, as said below
- offset_classes: int32 [128, 32], P(('rep', 'branch', 'dap')), parts along dimension 0, may hold values from 0 to 65
- couple_matrix: bfloat16 [128, 32, 128], P(('rep', 'branch', 'dap')), parts along dimension 0, may hold values from -6 to 6
- homolog_standardizer_factor: float32 [256], replicated, may hold values from 0.25 to 1.75
- first_factor_projector: bfloat16 [256, 32], replicated, may hold values from -0.375 to 0.375
- second_factor_projector: bfloat16 [256, 32], replicated, may hold values from -0.375 to 0.375
- product_final_projector: bfloat16 [1024, 128], replicated, may hold values from -0.1875 to 0.1875
- offset_embedding_matrix: bfloat16 [66, 128], replicated, may hold values from -6 to 6
- couple_standardizer_factor: float32 [128], replicated, may hold values from 0.25 to 1.75
- trilateral_edge_projectors: bfloat16 [128, 512], replicated, may hold values from -0.5 to 0.5
- trilateral_sigmoid_projector: bfloat16 [128, 128], replicated, may hold values from -0.5 to 0.5
- trilateral_final_projector: bfloat16 [128, 128], replicated, may hold values from -0.5 to 0.5
- trilateral_standardizer_factor: float32 [128], replicated, may hold values from 0.25 to 1.75
Outputs:
- pair_out: bfloat16 [128, 32, 128], P(('rep', 'branch', 'dap')), parts along dimension 0
The draws below stay inside these ranges and needn't reach their ends.
There are 4 independent parts, one for each index of `rep`. The reference program is written for one: setup_inputs(seed, part) draws one part's arguments, and reference() takes and returns one part's arrays. A program takes and returns all parts, laid end to end along the dimension named above; an argument that names none is the same for every part. Nothing has to cross between parts.
Inputs may be any that keep to these rules, and one draw needn't show every extreme that they name: `amino_validity_flags`: 0 or 1; exactly 12 residues are 0, at any positions.
All inputs are finite; a program needn't handle non-finite values. No bound on the sum of `homolog_validity_flags` on one device may be relied on, other than what follows from the above.
Results may differ from the reference program's by a relative error of at most 0.0036.
Values may be sent and summed in bfloat16 or wider, within the bound.
A program may use at most 64 MiB of HBM per device.

```python
import jax
import jax.numpy as jnp
from jax import lax

FEATURE_DEPTH = 256
CZ = 128
PRODUCT_DEPTH = 32
NBINS = 66
HOMOLOG_TOTAL = 128
AMINO_TOTAL = 32


def draw_amino_validity_flags(key, part):
    order = jax.random.permutation(jax.random.fold_in(key, 7103), AMINO_TOTAL)
    padded = 3 * AMINO_TOTAL // 8
    return (order >= padded).astype(jnp.int32)


def plant(array, stream_key, least, largest):
    extent = array.shape
    spot = [jax.random.randint(jax.random.fold_in(stream_key, axis), (), 0, extent[axis]) for axis in range(len(extent))]
    array = array.at[tuple(spot)].set(least)
    longest = extent.index(max(extent))
    spot[longest] = (spot[longest] + 1) % extent[longest]
    return array.at[tuple(spot)].set(largest)


def levels(stream_key, extent, split, smallest, largest):
    def one(dim, shards_of):
        steps = jax.random.uniform(jax.random.fold_in(jax.random.fold_in(stream_key, 6), dim), (shards_of,), jnp.float32, smallest / len(split), largest / len(split))
        return jnp.repeat(jnp.exp(steps), extent[dim] // shards_of).reshape((-1,) + (1,) * (len(extent) - dim - 1))

    level = one(*split[0])
    for cut in split[1:]:
        level = level * one(*cut)
    return level


def bell_draw(rng, extent, deviation, most, shards=(), held_as=jnp.bfloat16):
    result = deviation * jax.random.normal(rng, extent, jnp.float32)
    if shards:
        result = result * levels(rng, extent, shards, -0.22, 0.18)
    return jnp.clip(result, -most, most).astype(held_as)


def setup_inputs(seed: int = 0, part: int = 0) -> dict:
    keys = jax.random.split(jax.random.key(seed), 16)
    own_keys = jax.random.split(jax.random.fold_in(keys[15], part), 16)
    homolog_stack = bell_draw(own_keys[0], (HOMOLOG_TOTAL, AMINO_TOTAL, FEATURE_DEPTH), 1.0, 6.0, ((0, 8),))
    homolog_validity_flags = plant((jax.random.randint(own_keys[1], (HOMOLOG_TOTAL,), 0, 4) < 3).astype(jnp.int32), jax.random.fold_in(own_keys[1], 1), 0, 1)
    amino_validity_flags = draw_amino_validity_flags(jax.random.fold_in(jax.random.fold_in(keys[15], part), 71), part)
    offset_classes = plant(jax.random.randint(own_keys[3], (AMINO_TOTAL, AMINO_TOTAL), 0, NBINS), jax.random.fold_in(own_keys[3], 1), 0, NBINS - 1).astype(jnp.int32)
    couple_matrix = bell_draw(own_keys[4], (AMINO_TOTAL, AMINO_TOTAL, CZ), 1.0, 6.0, ((0, 8),))
    homolog_standardizer_factor = jnp.clip(1.0 + 0.15 * jax.random.normal(keys[5], (FEATURE_DEPTH,), jnp.float32), 0.25, 1.75)
    first_factor_projector = bell_draw(keys[6], (FEATURE_DEPTH, PRODUCT_DEPTH), FEATURE_DEPTH ** -0.5, 0.375)
    second_factor_projector = bell_draw(keys[7], (FEATURE_DEPTH, PRODUCT_DEPTH), FEATURE_DEPTH ** -0.5, 0.375)
    product_final_projector = bell_draw(keys[8], (PRODUCT_DEPTH * PRODUCT_DEPTH, CZ), (PRODUCT_DEPTH * PRODUCT_DEPTH) ** -0.5, 0.1875)
    offset_embedding_matrix = bell_draw(keys[9], (NBINS, CZ), 1.0, 6.0)
    couple_standardizer_factor = jnp.clip(1.0 + 0.15 * jax.random.normal(keys[10], (CZ,), jnp.float32), 0.25, 1.75)
    trilateral_edge_projectors = bell_draw(keys[11], (CZ, 4 * CZ), CZ ** -0.5, 0.5)
    trilateral_sigmoid_projector = bell_draw(keys[12], (CZ, CZ), CZ ** -0.5, 0.5)
    trilateral_final_projector = bell_draw(keys[13], (CZ, CZ), CZ ** -0.5, 0.5)
    trilateral_standardizer_factor = jnp.clip(1.0 + 0.15 * jax.random.normal(keys[14], (CZ,), jnp.float32), 0.25, 1.75)
    return dict(homolog_stack=homolog_stack, homolog_validity_flags=homolog_validity_flags, amino_validity_flags=amino_validity_flags, offset_classes=offset_classes, couple_matrix=couple_matrix, homolog_standardizer_factor=homolog_standardizer_factor, first_factor_projector=first_factor_projector, second_factor_projector=second_factor_projector, product_final_projector=product_final_projector, offset_embedding_matrix=offset_embedding_matrix, couple_standardizer_factor=couple_standardizer_factor, trilateral_edge_projectors=trilateral_edge_projectors, trilateral_sigmoid_projector=trilateral_sigmoid_projector, trilateral_final_projector=trilateral_final_projector, trilateral_standardizer_factor=trilateral_standardizer_factor)


def standardize_features(values, gain):
    mean = lax.optimization_barrier(jnp.mean(values, axis=-1, keepdims=True))
    centred = values - mean
    spread = lax.optimization_barrier(jnp.mean(centred * centred, axis=-1, keepdims=True))
    return centred * lax.rsqrt(spread + 1e-05) * gain

def reference(homolog_stack, homolog_validity_flags, amino_validity_flags, offset_classes, couple_matrix, homolog_standardizer_factor, first_factor_projector, second_factor_projector, product_final_projector, offset_embedding_matrix, couple_standardizer_factor, trilateral_edge_projectors, trilateral_sigmoid_projector, trilateral_final_projector, trilateral_standardizer_factor):
    plain_real_kind = jnp.float32
    standardized_source = standardize_features(homolog_stack.astype(plain_real_kind), homolog_standardizer_factor).astype(jnp.bfloat16)
    res_all = amino_validity_flags.astype(plain_real_kind)
    rows_live = homolog_validity_flags.astype(plain_real_kind)
    live = rows_live[:, None] * res_all[None, :]
    left = (jnp.einsum('src,cd->srd', standardized_source.astype(plain_real_kind), first_factor_projector.astype(plain_real_kind)) * live[:, :, None]).astype(jnp.bfloat16)
    right = (jnp.einsum('src,cd->srd', standardized_source.astype(plain_real_kind), second_factor_projector.astype(plain_real_kind)) * live[:, :, None]).astype(jnp.bfloat16)
    outer = jnp.einsum('sic,sje->ijce', left.astype(plain_real_kind), right.astype(plain_real_kind))
    amino_total = couple_matrix.shape[0]
    width = couple_matrix.shape[2]
    inner = first_factor_projector.shape[1]
    projected = jnp.dot(outer.reshape(amino_total * amino_total, inner * inner), product_final_projector.astype(plain_real_kind), precision=lax.Precision.HIGHEST).reshape(amino_total, amino_total, width)
    pair_live = res_all[:, None] * res_all[None, :]
    count = jnp.maximum(jnp.sum(rows_live) * pair_live, 1.0)
    onehot = (offset_classes[..., None] == jnp.arange(offset_embedding_matrix.shape[0], dtype=jnp.int32)).astype(plain_real_kind)
    embed = jnp.einsum('ijb,bc->ijc', onehot, offset_embedding_matrix.astype(plain_real_kind))
    updated = couple_matrix.astype(plain_real_kind) + embed + projected / count[..., None]
    normed_pair = standardize_features(updated, couple_standardizer_factor).astype(jnp.bfloat16)
    four = jnp.einsum('ijc,cd->ijd', normed_pair.astype(plain_real_kind), trilateral_edge_projectors.astype(plain_real_kind))
    tri_left = (jax.nn.sigmoid(four[..., :width]) * four[..., width:2 * width] * pair_live[..., None]).astype(jnp.bfloat16)
    tri_right = (jax.nn.sigmoid(four[..., 2 * width:3 * width]) * four[..., 3 * width:] * pair_live[..., None]).astype(jnp.bfloat16)
    triangle = jnp.einsum('ikc,jkc->ijc', tri_left.astype(plain_real_kind), tri_right.astype(plain_real_kind))
    triangle_normed = standardize_features(triangle, trilateral_standardizer_factor).astype(jnp.bfloat16)
    gate = jax.nn.sigmoid(jnp.einsum('ijc,cd->ijd', normed_pair.astype(plain_real_kind), trilateral_sigmoid_projector.astype(plain_real_kind)))
    change = jnp.einsum('ijc,cd->ijd', triangle_normed.astype(plain_real_kind), trilateral_final_projector.astype(plain_real_kind))
    return (updated + gate * change).astype(jnp.bfloat16)
```

```python
import functools

import jax
import jax.numpy as jnp
from jax import lax
from jax.experimental import pallas as pl
from jax.experimental.pallas import tpu as pltpu
from jax.sharding import PartitionSpec as P

F32 = jnp.float32
BF16 = jnp.bfloat16
MESH = pl.DeviceIdType.MESH
OPERANDS = 15
LANES = 128
SUB = 8


def iota(shape, axis):
    return lax.broadcasted_iota(jnp.int32, shape, axis)


def dot(a, b):
    return jnp.dot(a, b, preferred_element_type=F32)


def standardize(values, gain):
    mean = jnp.mean(values, axis=-1, keepdims=True)
    centred = values - mean
    spread = jnp.mean(centred * centred, axis=-1, keepdims=True)
    return centred * lax.rsqrt(spread + 1e-05) * gain


def kernel(
    nb, nz,
    *refs,
):
    operands, out_ref, held = refs[:OPERANDS], refs[OPERANDS], refs[OPERANDS + 1 : 2 * OPERANDS + 1]
    in_sem, *scratch = refs[2 * OPERANDS + 1 :]
    (x_ref, hflag_ref, aflag_ref, class_ref, couple_ref, hgain_ref, wl_ref, wr_ref, wout_ref,
     embed_ref, cgain_ref, wedge_ref, wgate_ref, wfin_ref, tgain_ref) = held
    (
    flag_all, right_all, left_send, left_all, tri_all, y_left, outer_buf, w_wide, w_perm, tri_buf, mix_buf,
    flag_ssem, flag_rsem, right_ssem, right_rsem, right_fsem, left_ssem, left_rsem,
    tri_ssem, tri_rsem, tri_fsem,
    ) = scratch
    n = nb * nz
    branch = lax.axis_index("branch")
    dap = lax.axis_index("dap")
    me = branch * nz + dap
    amino = aflag_ref.shape[1]
    seqs = hflag_ref.shape[1]
    rows = class_ref.shape[0]
    inner = wl_ref.shape[0]
    width = couple_ref.shape[1]
    reps = LANES // inner
    live = amino - 3 * amino // 8
    groups = live // reps
    pairs = rows * amino
    padded = -(-live // SUB) * SUB
    first = me * rows

    low = 2 * dap < nz
    same = [
        (branch, jnp.where(low, k + (k >= dap), nz - 1 - k - (nz - 1 - k <= dap))) for k in range(nz - 1)
    ]
    here = [(lax.rem(branch + step, nb), dap) for step in range(1, nb)]
    far = [(b[0], z[1]) for b in here for z in same]
    near = same + here
    everyone = near + far

    def index_of(peer):
        return peer[0] * nz + peer[1]

    def target(peer):
        return {"branch": peer[0], "dap": peer[1]}

    barrier = pltpu.get_barrier_semaphore()
    for peer in everyone:
        pl.semaphore_signal(barrier, inc=1, device_id=target(peer), device_id_type=MESH)

    loads = {}
    for k in (2, 1, 0, 5, 6, 7, 8, 3, 4, 9, 10, 11, 12, 13, 14):
        loads[k] = pltpu.make_async_copy(operands[k], held[k], in_sem.at[k])
        loads[k].start()

    loads[2].wait()
    loads[1].wait()
    aflag = jnp.broadcast_to(aflag_ref[...].astype(F32), (SUB, amino)).astype(BF16)
    hflag32 = hflag_ref[...].astype(F32)
    hflag = jnp.broadcast_to(hflag32, (SUB, seqs)).astype(BF16)

    def lane_keys(lanes):
        r = iota((amino, lanes), 0)
        k = lax.rem(iota((amino, lanes), 1), amino)
        count = dot(aflag, (r <= k).astype(BF16))
        alive = dot(aflag, (r == k).astype(BF16))
        return (count * alive)[0:1, :]

    flag_all[me] = jnp.broadcast_to(jnp.sum(hflag32, axis=1, keepdims=True), (1, LANES))

    total = seqs * amino
    key_x = lane_keys(total)
    hlane = dot(hflag, (iota((seqs, total), 0) == iota((seqs, total), 1) // amino).astype(BF16))[0:1, :]
    key_x = jnp.where(hlane > 0.5, key_x, 0.0).astype(jnp.int32)
    m_row = iota((live * seqs, 1), 0)
    same_seq = lax.rem(m_row, seqs) == iota((1, total), 1) // amino
    gather_right = jnp.where((key_x == m_row // seqs + 1) & same_seq, 1.0, 0.0).astype(BF16)
    lane_group = iota((1, LANES), 1) // inner
    alane = dot(
        aflag,
        (iota((amino, amino * inner), 0) == iota((amino, amino * inner), 1) // inner).astype(BF16),
    )[0:1, :]

    for k in (0, 5, 6, 7):
        loads[k].wait()
    normed = standardize(x_ref[...].astype(F32), hgain_ref[...]).astype(BF16)
    w_both = jnp.concatenate([wl_ref[...]] * reps + [wr_ref[...]] * reps, axis=0)
    sides = lax.dot_general(
        normed, w_both, (((1,), (1,)), ((), ())), preferred_element_type=F32
    )
    y_left[...] = sides[:, :LANES]
    right_rows = dot(gather_right, sides[:, LANES:].astype(BF16))
    for q in range(groups):
        block = right_rows[q * reps * seqs : (q * reps + 1) * seqs]
        for g in range(1, reps):
            start = (q * reps + g) * seqs
            block = jnp.where(lane_group == g, right_rows[start : start + seqs], block)
        right_all[me, :, q * LANES : (q + 1) * LANES] = block.astype(BF16)
    for d in range(n):
        block = y_left[pl.ds(d * rows, seqs, stride=amino), :]
        for g in range(1, rows):
            block = jnp.where(
                lane_group == g, y_left[pl.ds(d * rows + g, seqs, stride=amino), :], block
            )
        left_send[d] = (block * alane[:, d * LANES : (d + 1) * LANES]).astype(BF16)

    pl.semaphore_wait(barrier, n - 1)

    sends = []

    def push(src, dst, ssem, rsem, peer):
        copy = pltpu.make_async_remote_copy(
            src_ref=src, dst_ref=dst, send_sem=ssem, recv_sem=rsem,
            device_id=target(peer), device_id_type=MESH,
        )
        copy.start()
        sends.append(copy)

    def arrived(ref, slot, rsem):
        pltpu.make_async_remote_copy(
            src_ref=ref.at[slot], dst_ref=ref.at[slot], send_sem=rsem.at[slot],
            recv_sem=rsem.at[slot], device_id=target(everyone[0]), device_id_type=MESH,
        ).wait_recv()

    def push_left(peer):
        d = index_of(peer)
        push(left_send.at[d], left_all.at[me], left_ssem.at[d], left_rsem.at[me], peer)
        push(flag_all.at[me], flag_all.at[me], flag_ssem.at[d], flag_rsem.at[me], peer)

    def push_right(peer):
        push(right_all.at[me], right_all.at[me], right_ssem.at[index_of(peer)], right_rsem.at[me], peer)

    push_right(here[0])
    push_left(here[0])
    for peer, other in reversed(list(zip(same, far))):
        push_right(peer)
        push_left(peer)
        push_left(other)
    left_all[me] = left_send[me]

    for k in (8, 3, 4, 9, 10, 11, 12, 13, 14):
        loads[k].wait()
    w_wide[...] = wout_ref[...].astype(F32)
    for e in range(inner):
        w_perm[e * inner : (e + 1) * inner, :] = w_wide[
            pl.ds(e, inner, stride=inner), :
        ].astype(BF16)
    eye = iota((amino, amino), 0) == iota((amino, amino), 1)
    bins = embed_ref.shape[0]
    hot = []
    for i in range(rows):
        column = jnp.sum(
            jnp.where(eye, class_ref[i : i + 1, :], 0).astype(F32), axis=1, keepdims=True
        ).astype(jnp.int32)
        hot.append(jnp.where(column == iota((amino, bins), 1), 1.0, 0.0))
    onehot = jnp.concatenate(hot, axis=0).astype(BF16)
    base = couple_ref[...].astype(F32) + dot(onehot, embed_ref[...])

    key_pair = lane_keys(pairs)
    ilane = dot(
        aflag, (iota((amino, pairs), 0) == first + iota((amino, pairs), 1) // amino).astype(BF16)
    )[0:1, :]
    key_pair = jnp.where(ilane > 0.5, key_pair, 0.0).astype(jnp.int32)
    pair_row = iota((1, pairs), 1) // amino
    sel_rows = live * rows
    slots = rows * padded
    slot = iota((slots, 1), 0)
    gather = jnp.where(
        (key_pair == lax.rem(slot, padded) + 1) & (pair_row == slot // padded), 1.0, 0.0
    ).astype(BF16)
    base_c = dot(gather, couple_ref[...]) + dot(dot(gather, onehot).astype(BF16), embed_ref[...])
    sel_m = iota((sel_rows, 1), 0)
    lane_slot = iota((1, slots), 1)
    select_left = jnp.concatenate(
        [
            jnp.where(lane_slot == sel_m // rows + i * padded, 1.0, 0.0)
            for i in range(rows)
        ],
        axis=0,
    ).astype(BF16)
    wide_key = jnp.broadcast_to(lane_keys(amino), (amino, amino))
    key_col = jnp.sum(jnp.where(eye, wide_key, 0.0), axis=1, keepdims=True).astype(jnp.int32)
    key_col = jnp.concatenate([key_col] * rows, axis=0)
    col = iota((pairs, slots), 1)
    expand = jnp.where(
        (key_col == lax.rem(col, padded) + 1) & (iota((pairs, slots), 0) // amino == col // padded),
        1.0,
        0.0,
    ).astype(BF16)
    expand = jnp.concatenate([expand, expand], axis=1)
    if padded > live:
        outer_buf[live * inner :, :] = jnp.zeros(((padded - live) * inner, LANES), F32)

    for peer in same:
        slot = index_of(peer)
        arrived(right_all, slot, right_rsem)
        for k, other in enumerate(here):
            push(right_all.at[slot], right_all.at[slot], right_fsem.at[k, peer[1]], right_rsem.at[slot], other)
    for peer in everyone:
        arrived(left_all, index_of(peer), left_rsem)
        arrived(flag_all, index_of(peer), flag_rsem)
    for peer in here + far:
        arrived(right_all, index_of(peer), right_rsem)

    number = jnp.maximum(jnp.sum(flag_all[...], axis=0), 1.0)
    left = left_all[...].reshape(n * seqs, LANES)
    right = right_all[...].reshape(n * seqs, live * inner)
    outer_buf[: live * inner, :] = lax.dot_general(
        right, left, (((0,), (0,)), ((), ())), preferred_element_type=F32
    )
    parts = [[] for _ in range(rows)]
    lane = iota((1, LANES), 1)
    for q in range(inner // reps):
        block = [outer_buf[pl.ds(q * reps + g, padded, stride=inner), :] for g in range(reps)]
        span = reps // 2
        while span:
            upper = (lane // (span * inner)) % 2 == 1
            new = list(block)
            for a in range(reps):
                if a & span:
                    continue
                b = a | span
                shift = span * inner
                new[a] = jnp.where(upper, pltpu.roll(block[b], shift, 1), block[a])
                new[b] = jnp.where(upper, block[b], pltpu.roll(block[a], LANES - shift, 1))
            block = new
            span //= 2
        for i in range(rows):
            parts[i].append(block[i])
    packed = jnp.concatenate([jnp.concatenate(p, axis=1) for p in parts], axis=0).astype(BF16)
    product = dot(packed, w_perm[...])
    product = product / number
    pair_c = standardize(base_c + product, cgain_ref[...]).astype(BF16)
    right_two = dot(pair_c, wedge_ref[:, 2 * width :])
    tri_right = jax.nn.sigmoid(right_two[:, :width]) * right_two[:, width:]
    for i in range(rows):
        mix_buf[pl.ds(i, padded, stride=rows), :] = tri_right[i * padded : (i + 1) * padded]
    tri_all[me] = mix_buf[:sel_rows, :].astype(BF16)
    for peer in here + same[::-1]:
        push(tri_all.at[me], tri_all.at[me], tri_ssem.at[index_of(peer)], tri_rsem.at[me], peer)

    left_two = dot(pair_c, wedge_ref[:, : 2 * width])
    tri_left = (jax.nn.sigmoid(left_two[:, :width]) * left_two[:, width:]).astype(BF16)
    spread_left = dot(select_left, tri_left)
    high = product.astype(BF16)
    low_part = (product - high.astype(F32)).astype(BF16)
    updated = base + dot(expand, jnp.concatenate([high, low_part], axis=0))
    pair = standardize(updated, cgain_ref[...]).astype(BF16)
    gate = jax.nn.sigmoid(dot(pair, wgate_ref[...]))

    def passing(peer):
        slot = index_of(peer)
        arrived(tri_all, slot, tri_rsem)
        for k, other in enumerate(here):
            push(tri_all.at[slot], tri_all.at[slot], tri_fsem.at[k, peer[1]], tri_rsem.at[slot], other)

    pieces = SUB // rows
    sub = iota((SUB, LANES), 0)

    def triangle(start):
        blocks = [tri_all[start + h].astype(F32) for h in range(pieces)]
        for i in range(rows):
            mine = spread_left[i * sel_rows : (i + 1) * sel_rows]
            result = None
            for h in range(pieces):
                both = mine * blocks[h]
                acc = jnp.sum(both.reshape(sel_rows // SUB, SUB, LANES), axis=0)
                step = rows
                while step < SUB:
                    acc = acc + pltpu.roll(acc, step, 0)
                    step *= 2
                result = acc if result is None else jnp.where(sub // rows == h, acc, result)
            row = i * amino + start * rows
            tri_buf[pl.ds(row if isinstance(row, int) else pl.multiple_of(row, SUB), SUB), :] = result

    for peer in same:
        passing(peer)
    if nz % pieces == 0:
        for b in [branch] + [o[0] for o in here]:
            if b is not branch:
                for peer in here + far:
                    if peer[0] is b:
                        arrived(tri_all, index_of(peer), tri_rsem)
            for z in range(0, nz, pieces):
                triangle(b * nz + z)
    else:
        for peer in here + far:
            arrived(tri_all, index_of(peer), tri_rsem)
        for d in range(0, n, pieces):
            triangle(d)
    tri = standardize(tri_buf[...], tgain_ref[...]).astype(BF16)
    out_ref[...] = (updated + gate * dot(tri, wfin_ref[...])).astype(BF16)
    for copy in sends:
        copy.wait_send()


def on_device(nb, nz, x, hflags, aflags, classes, couple, hgain, wl, wr, wout, embed, cgain, wedge, wgate, wfin, tgain):
    n = nb * nz
    seqs, amino, depth = x.shape
    rows, _, width = couple.shape
    inner = wl.shape[1]
    live = amino - 3 * amino // 8
    padded = -(-live // SUB) * SUB
    dma = pltpu.SemaphoreType.DMA
    operands = (
        x.reshape(seqs * amino, depth), hflags.reshape(1, seqs), aflags.reshape(1, amino), classes,
        couple.reshape(rows * amino, width), hgain.reshape(1, depth), wl.T, wr.T, wout, embed,
        cgain.reshape(1, width), wedge, wgate, wfin, tgain.reshape(1, width),
    )
    out = pl.pallas_call(
        functools.partial(kernel, nb, nz),
        out_shape=pltpu.VMEM((rows * amino, width), BF16),
        in_specs=[pl.BlockSpec(memory_space=pl.ANY)] * OPERANDS,
        out_specs=pl.BlockSpec(memory_space=pltpu.VMEM),
        scratch_shapes=[pltpu.VMEM(a.shape, a.dtype) for a in operands]
        + [
            dma((OPERANDS,)),
            pltpu.VMEM((n, 1, LANES), F32),
            pltpu.VMEM((n, seqs, live * inner), BF16),
            pltpu.VMEM((n, seqs, LANES), BF16),
            pltpu.VMEM((n, seqs, LANES), BF16),
            pltpu.VMEM((n, live * rows, width), BF16),
            pltpu.VMEM((seqs * amino, LANES), F32),
            pltpu.VMEM((padded * inner, LANES), F32),
            pltpu.VMEM((inner * inner, width), F32),
            pltpu.VMEM((inner * inner, width), BF16),
            pltpu.VMEM((rows * amino, width), F32),
            pltpu.VMEM((rows * padded, width), F32),
            dma((n,)), dma((n,)),
            dma((n,)), dma((n,)), dma((nb, nz)),
            dma((n,)), dma((n,)),
            dma((n,)), dma((n,)), dma((nb, nz)),
        ],
        compiler_params=pltpu.CompilerParams(collective_id=0, has_side_effects=True),
    )(*operands)
    return out.reshape(rows, amino, width)


def solution(mesh):
    split = ("rep", "branch", "dap")
    placed = (
        P(split, None, None), P(split), P("rep"), P(split, None), P(split, None, None),
        P(), P(), P(), P(), P(), P(), P(), P(), P(), P(),
    )
    return jax.shard_map(
        functools.partial(on_device, mesh.shape["branch"], mesh.shape["dap"]),
        mesh=mesh,
        in_specs=placed,
        out_specs=P(split, None, None),
        check_vma=False,
    )
```

```python
import functools

import jax
import jax.numpy as jnp
from jax import lax
from jax.experimental import pallas as pl
from jax.experimental.pallas import tpu as pltpu
from jax.sharding import PartitionSpec as P

F32 = jnp.float32
BF16 = jnp.bfloat16
MESH = pl.DeviceIdType.MESH
OPERANDS = 15
LANES = 128
SUB = 8


def iota(shape, axis):
    return lax.broadcasted_iota(jnp.int32, shape, axis)


def dot(a, b):
    return jnp.dot(a, b, preferred_element_type=F32)


def standardize(values, gain):
    mean = jnp.mean(values, axis=-1, keepdims=True)
    centred = values - mean
    spread = jnp.mean(centred * centred, axis=-1, keepdims=True)
    return centred * lax.rsqrt(spread + 1e-05) * gain


def kernel(
    nb, nz,
    *refs,
):
    operands, out_ref, held = refs[:OPERANDS], refs[OPERANDS], refs[OPERANDS + 1 : 2 * OPERANDS + 1]
    in_sem, *scratch = refs[2 * OPERANDS + 1 :]
    (x_ref, hflag_ref, aflag_ref, class_all, couple_all, hgain_ref, wl_ref, wr_ref, wout_ref,
     embed_ref, cgain_ref, wedge_ref, wgate_ref, wfin_ref, tgain_ref) = held
    (
    flag_all, right_send, right_main, right_tail, left_send, left_all, left_last, tri_all, y_left, outer_buf,
    base_buf, base_send, base_last, product_all, edge_buf, spread_buf, own_buf, part_send, part_in, tri_buf,
    flag_sems, right_sems, tail_sems, left_sems, last_sems, base_sems, tri_ssem, tri_rsem, part_ssem, part_rsem,
    pair_ssem, pair_rsem, ready,
    ) = scratch
    n = nb * nz
    branch = lax.axis_index("branch")
    dap = lax.axis_index("dap")
    me = branch * nz + dap
    amino = aflag_ref.shape[1]
    seqs = hflag_ref.shape[1]
    rows = class_all.shape[1]
    inner = wl_ref.shape[0]
    width = couple_all.shape[2]
    reps = LANES // inner
    live = amino - 3 * amino // 8
    tiles = live // reps
    groups = -(-tiles // nb)
    even = tiles % nb == 0
    part = groups * reps
    main = (groups - 1) * LANES
    block_rows = nb * rows
    slots = part * block_rows
    firm = slots - reps * block_rows
    pairs = rows * amino
    chips = [k + (k >= dap) for k in range(nz - 1)]
    redo = nz > 2
    end = nz - 1
    order = []
    for k in range(nz - 1):
        rank = jnp.where(dap == 0, nz - 2, jnp.where(dap == end, end, dap - 1))
        rank = k + (k >= rank)
        order.append(jnp.where(rank < nz - 2, rank + 1, jnp.where(rank == nz - 2, 0, end)))
    other = nb - 1 - branch
    partner = (other, dap)
    everyone = [partner] + [(b, z) for z in chips for b in (branch, other)]

    def index_of(peer):
        return peer[0] * nz + peer[1]

    def target(peer):
        return {"branch": peer[0], "dap": peer[1]}

    barrier = pltpu.get_barrier_semaphore()
    pl.semaphore_signal(barrier, inc=1, device_id=target(partner), device_id_type=MESH)
    for b, z in everyone[1:]:

        @pl.when(z > dap)
        def _():
            pl.semaphore_signal(barrier, inc=1, device_id=target((b, z)), device_id_type=MESH)

    loads = {}
    for k in (2, 1, 0, 5, 6, 7, 8, 3, 4, 9, 10, 11, 12, 13, 14):
        place = held[k].at[branch] if k in (3, 4) else held[k]
        loads[k] = pltpu.make_async_copy(operands[k], place, in_sem.at[k])
        loads[k].start()

    pl.semaphore_wait(barrier, dap * nb + 1)
    for b, z in everyone[1:]:

        @pl.when(z < dap)
        def _():
            pl.semaphore_signal(ready.at[dap], inc=1, device_id=target((b, z)), device_id_type=MESH)

    if not even:

        @pl.when(branch > 0)
        def _():
            right_tail[...] = jnp.zeros(right_tail.shape, BF16)
            tri_all[:, firm:, :] = jnp.zeros((nz, slots - firm, width), BF16)

    loads[2].wait()
    loads[1].wait()
    aflag = jnp.broadcast_to(aflag_ref[...].astype(F32), (SUB, amino)).astype(BF16)
    hflag32 = hflag_ref[...].astype(F32)
    hflag = jnp.broadcast_to(hflag32, (SUB, seqs)).astype(BF16)

    def lane_keys(lanes):
        r = iota((amino, lanes), 0)
        k = lax.rem(iota((amino, lanes), 1), amino)
        count = dot(aflag, (r <= k).astype(BF16))
        alive = dot(aflag, (r == k).astype(BF16))
        return (count * alive)[0:1, :]

    flag_all[me] = jnp.broadcast_to(jnp.sum(hflag32, axis=1, keepdims=True), (1, LANES))

    total = seqs * amino
    key_x = lane_keys(total)
    hlane = dot(hflag, (iota((seqs, total), 0) == iota((seqs, total), 1) // amino).astype(BF16))[0:1, :]
    key_x = jnp.where(hlane > 0.5, key_x, 0.0).astype(jnp.int32)
    m_row = iota((live * seqs, 1), 0)
    same_seq = lax.rem(m_row, seqs) == iota((1, total), 1) // amino
    gather_right = jnp.where((key_x == m_row // seqs + 1) & same_seq, 1.0, 0.0).astype(BF16)
    lane_group = iota((1, LANES), 1) // inner
    alane = dot(
        aflag,
        (iota((amino, amino * inner), 0) == iota((amino, amino * inner), 1) // inner).astype(BF16),
    )[0:1, :]

    for k in (0, 5, 6, 7):
        loads[k].wait()
    normed = standardize(x_ref[...].astype(F32), hgain_ref[...]).astype(BF16)
    w_both = jnp.concatenate([wl_ref[...]] * reps + [wr_ref[...]] * reps, axis=0)
    sides = lax.dot_general(
        normed, w_both, (((1,), (1,)), ((), ())), preferred_element_type=F32
    )
    y_left[...] = sides[:, :LANES]
    right_rows = dot(gather_right, sides[:, LANES:].astype(BF16))
    for b in range(nb):
        for t in range(min(groups, tiles - b * groups)):
            begin = (b * part + t * reps) * seqs
            block = right_rows[begin : begin + seqs]
            for g in range(1, reps):
                block = jnp.where(
                    lane_group == g, right_rows[begin + g * seqs : begin + (g + 1) * seqs], block
                )
            right_send[b, t] = block.astype(BF16)
    for d in range(n):
        block = y_left[pl.ds(d * rows, seqs, stride=amino), :]
        for g in range(1, rows):
            block = jnp.where(
                lane_group == g, y_left[pl.ds(d * rows + g, seqs, stride=amino), :], block
            )
        left_send[d % nz, d // nz] = (block * alane[:, d * LANES : (d + 1) * LANES]).astype(BF16)


    def push(src, dst, ssem, rsem, peer, when=None):
        copy = pltpu.make_async_remote_copy(
            src_ref=src, dst_ref=dst, send_sem=ssem, recv_sem=rsem,
            device_id=target(peer), device_id_type=MESH,
        )
        guarded(when, copy.start)

    def tail(b):
        return None if even else b == 0

    def guarded(when, act):
        if when is None:
            act()
        else:
            pl.when(when)(act)

    def drain(ref, ssem, when=None):
        wait = pltpu.make_async_remote_copy(
            src_ref=ref, dst_ref=ref, send_sem=ssem, recv_sem=ssem,
            device_id=target(partner), device_id_type=MESH,
        ).wait_send
        guarded(when, wait)

    def arrived(ref, rsem, when=None):
        wait = pltpu.make_async_remote_copy(
            src_ref=ref, dst_ref=ref, send_sem=rsem,
            recv_sem=rsem, device_id=target(partner), device_id_type=MESH,
        ).wait_recv
        guarded(when, wait)

    def share(ref, k):
        push(ref.at[branch], ref.at[branch], pair_ssem.at[k], pair_rsem.at[k], partner)

    for k in (3, 4):
        loads[k].wait()
    def push_block(peer):
        b, z = peer
        push(left_send.at[z], left_all.at[me], left_sems.at[0], left_sems.at[1], peer)
        push(right_send.at[b, : groups - 1], right_main.at[me], right_sems.at[0], right_sems.at[1], peer)
        push(right_send.at[b, groups - 1], right_tail.at[me], tail_sems.at[0], tail_sems.at[1], peer, tail(b))
        push(flag_all.at[me], flag_all.at[me], flag_sems.at[0], flag_sems.at[1], peer)

    push_block(partner)
    share(class_all, 0)
    share(couple_all, 1)
    for z in order:

        @pl.when(z > dap)
        def _():
            pl.semaphore_wait(ready.at[z], nb)

        push_block((branch, z))
        push_block((other, z))
    if redo:
        push(left_send.at[end], left_last.at[me], last_sems.at[0], last_sems.at[1], (other, 0))
        push(left_send.at[end], left_last.at[me], last_sems.at[0], last_sems.at[1], (branch, 0), dap != 0)

        @pl.when(dap == 0)
        def _():
            left_last[me] = left_send[end]

    right_main[me] = right_send[branch, : groups - 1]
    if even:
        right_tail[me] = right_send[branch, groups - 1]
    else:

        @pl.when(branch == 0)
        def _():
            right_tail[me] = right_send[0, groups - 1]

    left_all[me] = left_send[dap]

    for k in (8, 9, 10, 11, 12, 13, 14):
        loads[k].wait()
    chip_pairs = nb * pairs
    lane_pair = iota((1, chip_pairs), 1)
    key_pair = lane_keys(chip_pairs)
    residue = (lane_pair // pairs * nz + dap) * rows + lax.rem(lane_pair // amino, rows)
    ilane = dot(aflag, (iota((amino, chip_pairs), 0) == residue).astype(BF16))[0:1, :]
    key_pair = jnp.where(ilane > 0.5, key_pair, 0.0).astype(jnp.int32)
    slot = iota((slots, 1), 0)
    gather = jnp.where(
        (key_pair == branch * part + slot // block_rows + 1) & (lane_pair // amino == lax.rem(slot, block_rows)),
        1.0,
        0.0,
    ).astype(BF16)
    eye = iota((amino, amino), 0) == iota((amino, amino), 1)
    wide_key = jnp.broadcast_to(lane_keys(amino), (amino, amino))
    key_col = jnp.sum(jnp.where(eye, wide_key, 0.0), axis=1, keepdims=True).astype(jnp.int32)
    key_col = jnp.concatenate([key_col] * rows, axis=0)
    col = iota((1, nb * slots), 1)
    expand = jnp.where(
        (key_col == col // block_rows + 1)
        & (iota((pairs, 1), 0) // amino + branch * rows == lax.rem(col, block_rows)),
        1.0,
        0.0,
    ).astype(BF16)
    expand = jnp.concatenate([expand, expand], axis=1)
    arrived(class_all.at[other], pair_rsem.at[0])
    arrived(couple_all.at[other], pair_rsem.at[1])
    bins = embed_ref.shape[0]
    hot = []
    for b in range(nb):
        for i in range(rows):
            column = jnp.sum(
                jnp.where(eye, class_all[b, i : i + 1, :], 0).astype(F32), axis=1, keepdims=True
            ).astype(jnp.int32)
            hot.append(jnp.where(column == iota((amino, bins), 1), 1.0, 0.0))
    onehot = jnp.concatenate(hot, axis=0).astype(BF16)
    couple = couple_all[...].reshape(chip_pairs, width)
    base_buf[...] = (couple.astype(F32) + dot(onehot, embed_ref[...])).reshape(nb, pairs, width)
    base_c = dot(gather, couple) + dot(dot(gather, onehot).astype(BF16), embed_ref[...])

    if redo:

        @pl.when(dap == end)
        def _():
            base_send[...] = base_c.astype(BF16)

        push(base_send, base_last, base_sems.at[0], base_sems.at[1], (branch, 0), dap == end)

    arrived(right_main.at[: n - 1], right_sems.at[1])
    arrived(right_tail.at[: n - 1], tail_sems.at[1], tail(branch))
    arrived(left_all.at[: n - 1], left_sems.at[1])
    arrived(flag_all.at[: n - 1], flag_sems.at[1])

    number = jnp.maximum(jnp.sum(flag_all[...], axis=0), 1.0)
    right = jnp.concatenate(
        [right_main[:, t].reshape(n * seqs, LANES) for t in range(groups - 1)]
        + [right_tail[...].reshape(n * seqs, LANES)],
        axis=1,
    )
    lane = iota((1, LANES), 1)

    def middle(left_ref, base):
        left = jnp.concatenate([left_ref[:, b].reshape(n * seqs, LANES) for b in range(nb)], axis=1)
        outer = lax.dot_general(left, right, (((0,), (0,)), ((), ())), preferred_element_type=F32)
        for t in range(groups):
            outer_buf[t] = outer[:, t * LANES : (t + 1) * LANES]
        parts = [[] for _ in range(part)]
        for t in range(groups):
            for q in range(inner // reps):
                block = [outer_buf[t, pl.ds(q * reps + g, block_rows, stride=inner), :] for g in range(reps)]
                span = reps // 2
                while span:
                    upper = (lane // (span * inner)) % 2 == 1
                    new = list(block)
                    for a in range(reps):
                        if a & span:
                            continue
                        b = a | span
                        shift = span * inner
                        new[a] = jnp.where(upper, pltpu.roll(block[b], shift, 1), block[a])
                        new[b] = jnp.where(upper, block[b], pltpu.roll(block[a], LANES - shift, 1))
                    block = new
                    span //= 2
                for g in range(reps):
                    parts[t * reps + g].append(block[g])
        packed = jnp.concatenate([jnp.concatenate(p, axis=1) for p in parts], axis=0).astype(BF16)
        product = dot(packed, wout_ref[...]) / number
        pair_c = standardize(base + product, cgain_ref[...]).astype(BF16)
        right_two = dot(pair_c, wedge_ref[:, 2 * width :])
        tri_right = jax.nn.sigmoid(right_two[:, :width]) * right_two[:, width:]
        return product, pair_c, tri_right.astype(BF16)

    product, pair_c, tri_all[dap] = middle(left_all, base_c)
    full = tail(branch)
    short = None if even else branch != 0

    def tri_block(z, size):
        return tri_all.at[z, :size]

    for z in chips:
        skip = redo & (dap == end) & (z == 0)
        if even:
            push(tri_all.at[dap], tri_all.at[dap], tri_ssem.at[0], tri_rsem.at[dap], (branch, z), ~skip)
        else:
            for size, when in ((slots, full), (firm, short)):
                push(
                    tri_block(dap, size), tri_block(dap, size), tri_ssem.at[0], tri_rsem.at[dap], (branch, z),
                    when & ~skip,
                )

    product_all[branch] = product
    share(product_all, 2)
    left_two = dot(pair_c, wedge_ref[:, : 2 * width])
    edge_buf[...] = (jax.nn.sigmoid(left_two[:, :width]) * left_two[:, width:]).astype(BF16).astype(F32)
    for i in range(block_rows):
        for k in range(part):
            row = edge_buf[k * block_rows + i : k * block_rows + i + 1, :]
            spread_buf[i, k * SUB : (k + 1) * SUB, :] = jnp.broadcast_to(row, (SUB, width))

    def triangle(z, side, store):
        block = tri_all[z].astype(F32)
        for i in range(rows):
            both = spread_buf[side * rows + i] * block
            store[z, i] = jnp.sum(both.reshape(part, SUB, width), axis=0)

    def contribute(z):
        triangle(z, other, part_send)
        push(part_send.at[z], part_in.at[z], part_ssem.at[0], part_rsem.at[z], partner)
        triangle(z, branch, own_buf)

    def settle(z):
        arrived(part_in.at[z], part_rsem.at[z])
        for i in range(rows):
            total = own_buf[z, i] + part_in[z, i]
            for b in range(nb):
                row = i * amino + (b * nz + z) * rows
                tri_buf[pl.ds(pl.multiple_of(row, rows), rows), :] = total[b * rows : (b + 1) * rows]

    contribute(dap)
    if redo:

        @pl.when(dap == 0)
        def _():
            arrived(left_last.at[: n - 1], last_sems.at[1])
            arrived(base_last, base_sems.at[1])
            tri_all[end] = middle(left_last, base_last[...].astype(F32))[2]
            contribute(end)

    late = [jnp.where(dap == 0, k + 1, (k + 1 + (k + 1 >= dap)) % nz) for k in range(nz - 1)]
    late = [jnp.where((dap == 0) | (k < nz - 2), z, 0) for k, z in enumerate(late)]
    for k, z in enumerate(late):
        skip = redo & (dap == 0) & (z == end)

        @pl.when(~skip)
        def _():
            if even:
                arrived(tri_all.at[z], tri_rsem.at[z])
            else:
                arrived(tri_block(z, slots), tri_rsem.at[z], full)
                arrived(tri_block(z, firm), tri_rsem.at[z], short)
            contribute(z)
    arrived(product_all.at[other], pair_rsem.at[2])
    whole = product_all[...].reshape(nb * slots, width)
    high = whole.astype(BF16)
    rest = (whole - high.astype(F32)).astype(BF16)
    updated = base_buf[branch] + dot(expand, jnp.concatenate([high, rest], axis=0))
    pair = standardize(updated, cgain_ref[...]).astype(BF16)
    gate = jax.nn.sigmoid(dot(pair, wgate_ref[...]))
    for z in [dap] + late:
        settle(z)
    tri = standardize(tri_buf[...], tgain_ref[...]).astype(BF16)
    out_ref[...] = (updated + gate * dot(tri, wfin_ref[...])).astype(BF16)
    drain(left_all.at[: n - 1], left_sems.at[0])
    drain(right_main.at[: n - 1], right_sems.at[0])
    if even:
        drain(right_tail.at[: n - 1], tail_sems.at[0])
    else:
        drain(right_tail.at[: nz - 1], tail_sems.at[0], full)
        drain(right_tail.at[:nz], tail_sems.at[0], short)
    drain(flag_all.at[: n - 1], flag_sems.at[0])
    if redo:
        drain(left_last.at[:1], last_sems.at[0], dap == 0)
        drain(left_last.at[:nb], last_sems.at[0], dap != 0)
        drain(base_send, base_sems.at[0], dap == end)
    for fewer, last in ((1, redo & (dap == end)), (0, ~(redo & (dap == end)))):
        if even:
            drain(tri_all.at[: nz - 1 - fewer], tri_ssem.at[0], last)
        else:
            drain(tri_all.at[: nz - 1 - fewer], tri_ssem.at[0], last & full)
            drain(tri_all.at[: nz - 1 - fewer, :firm], tri_ssem.at[0], last & short)
    drain(part_send, part_ssem.at[0])
    for k, ref in enumerate((class_all, couple_all, product_all)):
        drain(ref.at[branch], pair_ssem.at[k])


def on_device(nb, nz, x, hflags, aflags, classes, couple, hgain, wl, wr, wout, embed, cgain, wedge, wgate, wfin, tgain):
    n = nb * nz
    seqs, amino, depth = x.shape
    rows, _, width = couple.shape
    inner = wl.shape[1]
    live = amino - 3 * amino // 8
    groups = -(-(live // (LANES // inner)) // nb)
    part = groups * (LANES // inner)
    slots = part * nb * rows
    dma = pltpu.SemaphoreType.DMA
    operands = (
        x.reshape(seqs * amino, depth), hflags.reshape(1, seqs), aflags.reshape(1, amino), classes,
        couple.reshape(rows * amino, width), hgain.reshape(1, depth), wl.T, wr.T, wout, embed,
        cgain.reshape(1, width), wedge, wgate, wfin, tgain.reshape(1, width),
    )
    held = [pltpu.VMEM((nb, *a.shape) if k in (3, 4) else a.shape, a.dtype) for k, a in enumerate(operands)]
    out = pl.pallas_call(
        functools.partial(kernel, nb, nz),
        out_shape=pltpu.VMEM((rows * amino, width), BF16),
        in_specs=[pl.BlockSpec(memory_space=pl.ANY)] * OPERANDS,
        out_specs=pl.BlockSpec(memory_space=pltpu.VMEM),
        scratch_shapes=held
        + [
            dma((OPERANDS,)),
            pltpu.VMEM((n, 1, LANES), F32),
            pltpu.VMEM((nb, groups, seqs, LANES), BF16),
            pltpu.VMEM((n, groups - 1, seqs, LANES), BF16),
            pltpu.VMEM((n, seqs, LANES), BF16),
            pltpu.VMEM((nz, nb, seqs, LANES), BF16),
            pltpu.VMEM((n, nb, seqs, LANES), BF16),
            pltpu.VMEM((n, nb, seqs, LANES), BF16),
            pltpu.VMEM((nz, slots, width), BF16),
            pltpu.VMEM((seqs * amino, LANES), F32),
            pltpu.VMEM((groups, nb * LANES, LANES), F32),
            pltpu.VMEM((nb, rows * amino, width), F32),
            pltpu.VMEM((slots, width), BF16),
            pltpu.VMEM((slots, width), BF16),
            pltpu.VMEM((nb, slots, width), F32),
            pltpu.VMEM((slots, width), F32),
            pltpu.VMEM((nb * rows, slots, width), F32),
            pltpu.VMEM((nz, rows, SUB, width), F32),
            pltpu.VMEM((nz, rows, SUB, width), F32),
            pltpu.VMEM((nz, rows, SUB, width), F32),
            pltpu.VMEM((rows * amino, width), F32),
        ]
        + [dma((2,))] * 6
        + [dma((1,)), dma((nz,)), dma((1,)), dma((nz,)), dma((3,)), dma((3,))]
        + [pltpu.SemaphoreType.REGULAR((nz,))],
        compiler_params=pltpu.CompilerParams(collective_id=0, has_side_effects=True),
    )(*operands)
    return out.reshape(rows, amino, width)


def solution(mesh):
    split = ("rep", "branch", "dap")
    placed = (
        P(split, None, None), P(split), P("rep"), P(split, None), P(split, None, None),
        P(), P(), P(), P(), P(), P(), P(), P(), P(), P(),
    )
    return jax.shard_map(
        functools.partial(on_device, mesh.shape["branch"], mesh.shape["dap"]),
        mesh=mesh,
        in_specs=placed,
        out_specs=P(split, None, None),
        check_vma=False,
    )
```

```python
import functools

import jax
import jax.numpy as jnp
from jax import lax
from jax.experimental import pallas as pl
from jax.experimental.pallas import tpu as pltpu
from jax.sharding import PartitionSpec as P

F32 = jnp.float32
BF16 = jnp.bfloat16
MESH = pl.DeviceIdType.MESH
OPERANDS = 15
LANES = 128
SUB = 8


def iota(shape, axis):
    return lax.broadcasted_iota(jnp.int32, shape, axis)


def dot(a, b):
    return jnp.dot(a, b, preferred_element_type=F32)


def standardize(values, gain):
    mean = jnp.mean(values, axis=-1, keepdims=True)
    centred = values - mean
    spread = jnp.mean(centred * centred, axis=-1, keepdims=True)
    return centred * lax.rsqrt(spread + 1e-05) * gain


def kernel(
    nb, nz,
    *refs,
):
    operands, out_ref, held = refs[:OPERANDS], refs[OPERANDS], refs[OPERANDS + 1 : 2 * OPERANDS + 1]
    in_sem, *scratch = refs[2 * OPERANDS + 1 :]
    (x_ref, hflag_ref, aflag_ref, class_all, couple_all, hgain_ref, wl_ref, wr_ref, wout_ref,
     embed_ref, cgain_ref, wedge_ref, wgate_ref, wfin_ref, tgain_ref) = held
    (
    flag_all, right_send, right_all, left_send, left_all, left_last, tri_all, y_left, outer_buf,
    base_buf, base_send, base_last, product_all, edge_buf, spread_buf, own_buf, part_send, part_in, tri_buf, updated_buf, gate_buf,
    flag_sems, right_sems, pass_sems, last_sems, base_sems, left_rsem, tri_ssem, tri_rsem, part_ssem, part_rsem,
    pair_ssem, pair_rsem, ready,
    ) = scratch
    n = nb * nz
    branch = lax.axis_index("branch")
    dap = lax.axis_index("dap")
    me = branch * nz + dap
    amino = aflag_ref.shape[1]
    seqs = hflag_ref.shape[1]
    rows = class_all.shape[1]
    inner = wl_ref.shape[0]
    width = couple_all.shape[2]
    reps = LANES // inner
    live = amino - 3 * amino // 8
    tiles = live // reps
    groups = -(-tiles // nb)
    even = tiles % nb == 0
    part = groups * reps
    most = groups
    least = most if even else most - 1
    block_rows = nb * rows
    slots = part * block_rows
    firm = slots - reps * block_rows
    pairs = rows * amino
    side = nb - 1 - branch
    wide = nb - 1
    chips = [k + (k >= dap) for k in range(nz - 1)]
    redo = nz > 2
    end = nz - 1
    order = []
    for k in range(nz - 1):
        rank = jnp.where(dap == 0, nz - 2, jnp.where(dap == end, end, dap - 1))
        rank = k + (k >= rank)
        order.append(jnp.where(rank < nz - 2, rank + 1, jnp.where(rank == nz - 2, 0, end)))
    other = nb - 1 - branch
    partner = (other, dap)
    everyone = [partner] + [(b, z) for z in chips for b in (branch, other)]

    def index_of(peer):
        return peer[0] * nz + peer[1]

    def target(peer):
        return {"branch": peer[0], "dap": peer[1]}

    barrier = pltpu.get_barrier_semaphore()
    pl.semaphore_signal(barrier, inc=1, device_id=target(partner), device_id_type=MESH)
    for b, z in everyone[1:]:

        @pl.when(z > dap)
        def _():
            pl.semaphore_signal(barrier, inc=1, device_id=target((b, z)), device_id_type=MESH)

    loads = {}
    for k in (2,1,0,5,6,7,8,3,4,9,10,11,12,13,14):
        place = held[k].at[branch] if k in (3, 4) else held[k]
        loads[k] = pltpu.make_async_copy(operands[k], place, in_sem.at[k])
        if k == 0:
            step = x_ref.shape[0] // 8
            for j in range(8):
                piece = pl.ds(j * step, step)
                pltpu.make_async_copy(operands[0].at[piece], x_ref.at[piece], in_sem.at[0]).start()
        else:
            loads[k].start()

    pl.semaphore_wait(barrier, dap * nb + 1)
    for b, z in everyone[1:]:

        @pl.when(z < dap)
        def _():
            pl.semaphore_signal(ready.at[dap - 1], inc=1, device_id=target((b, z)), device_id_type=MESH)

    if not even:

        @pl.when(branch != wide)
        def _():
            right_all[:, least:] = jnp.zeros((n, most - least, seqs, LANES), BF16)
            tri_all[:, firm:, :] = jnp.zeros((nz, slots - firm, width), BF16)

    loads[2].wait()
    loads[1].wait()
    aflag = jnp.broadcast_to(aflag_ref[...].astype(F32), (SUB, amino)).astype(BF16)
    hflag32 = hflag_ref[...].astype(F32)
    hflag = jnp.broadcast_to(hflag32, (SUB, seqs)).astype(BF16)

    def lane_keys(lanes):
        r = iota((amino, lanes), 0)
        k = lax.rem(iota((amino, lanes), 1), amino)
        count = dot(aflag, (r <= k).astype(BF16))
        alive = dot(aflag, (r == k).astype(BF16))
        return (count * alive)[0:1, :]

    flag_all[me] = jnp.broadcast_to(jnp.sum(hflag32, axis=1, keepdims=True), (1, LANES))

    total = seqs * amino
    span = SUB * amino
    key_x = lane_keys(span)
    hlane = dot(hflag, (iota((seqs, total), 0) == iota((seqs, total), 1) // amino).astype(BF16))[0:1, :]
    gather_right = []
    for h in range(seqs // SUB):
        code = (key_x - 1.0) * SUB + (iota((1, span), 1) // amino).astype(F32)
        code = jnp.where(hlane[:, h * span : (h + 1) * span] * key_x > 0.5, code, -1.0).astype(jnp.int32)
        gather_right.append(jnp.where(iota((live * SUB, 1), 0) == code, 1.0, 0.0).astype(BF16))
    lane_group = iota((1, LANES), 1) // inner
    alane = dot(
        aflag,
        (iota((amino, amino * inner), 0) == iota((amino, amino * inner), 1) // inner).astype(BF16),
    )[0:1, :]

    for k in (0, 5, 6, 7):
        loads[k].wait()
    normed = standardize(x_ref[...].astype(F32), hgain_ref[...]).astype(BF16)
    w_both = jnp.concatenate([wl_ref[...]] * reps + [wr_ref[...]] * reps, axis=0)
    sides = lax.dot_general(
        normed, w_both, (((1,), (1,)), ((), ())), preferred_element_type=F32
    )
    for i in range(seqs):
        y_left[pl.ds(i * (amino + 1), amino), :] = sides[i * amino : (i + 1) * amino, :LANES]
    right_rows = [
        dot(gather, sides[h * span : (h + 1) * span, LANES:].astype(BF16)) for h, gather in enumerate(gather_right)
    ]

    def right_of(k):
        return jnp.concatenate([part_rows[k * SUB : (k + 1) * SUB] for part_rows in right_rows], axis=0)

    for b in range(nb):
        for t in range(min(groups, tiles - (nb - 1 - b) * groups)):
            begin = (nb - 1 - b) * part + t * reps
            block = right_of(begin)
            for g in range(1, reps):
                block = jnp.where(lane_group == g, right_of(begin + g), block)
            right_send[b, t] = block.astype(BF16)
    for d in range(n):
        block = y_left[pl.ds(d * rows, seqs, stride=amino + 1), :]
        for g in range(1, rows):
            block = jnp.where(
                lane_group == g, y_left[pl.ds(d * rows + g, seqs, stride=amino + 1), :], block
            )
        left_send[d % nz, d // nz] = (block * alane[:, d * LANES : (d + 1) * LANES]).astype(BF16)


    def push(src, dst, ssem, rsem, peer, when=None):
        copy = pltpu.make_async_remote_copy(
            src_ref=src, dst_ref=dst, send_sem=ssem, recv_sem=rsem,
            device_id=target(peer), device_id_type=MESH,
        )
        guarded(when, copy.start)

    def guarded(when, act):
        if when is None:
            act()
        else:
            pl.when(when)(act)

    def drain(ref, ssem, when=None):
        wait = pltpu.make_async_remote_copy(
            src_ref=ref, dst_ref=ref, send_sem=ssem, recv_sem=ssem,
            device_id=target(partner), device_id_type=MESH,
        ).wait_send
        guarded(when, wait)

    def arrived(ref, rsem, when=None):
        wait = pltpu.make_async_remote_copy(
            src_ref=ref, dst_ref=ref, send_sem=rsem,
            recv_sem=rsem, device_id=target(partner), device_id_type=MESH,
        ).wait_recv
        guarded(when, wait)

    def share(ref, k):
        push(ref.at[branch], ref.at[branch], pair_ssem.at[k], pair_rsem.at[k], partner)

    def push_right(b, z, when=None):
        size = most if even or b == wide else least
        push(
            right_send.at[b, :size], right_all.at[me, :size], right_sems.at[0], right_sems.at[1], (b, z), when
        )

    def push_left(z):
        push(left_send.at[z], left_all.at[me], pass_sems.at[0], left_rsem.at[dap], (branch, z))

    for z in order:

        @pl.when(z > dap)
        def _():
            pl.semaphore_wait(ready.at[z - 1], nb)

        push_left(z)
        if redo:
            push(left_send.at[end], left_last.at[me], last_sems.at[0], last_sems.at[1], (branch, 0), z == 0)
        for b in range(nb):
            push_right(b, z)
        for b in range(nb):
            push(flag_all.at[me], flag_all.at[me], flag_sems.at[0], flag_sems.at[1], (b, z))
    for b in range(nb):
        push_right(b, dap, branch != b)
    push(left_send.at[dap], left_all.at[me], pass_sems.at[0], pass_sems.at[1], partner)
    push(flag_all.at[me], flag_all.at[me], flag_sems.at[0], flag_sems.at[1], partner)
    for k in (3, 4):
        loads[k].wait()
    share(class_all, 0)
    share(couple_all, 1)
    left_all[me] = left_send[dap]
    right_all[me, :least] = right_send[branch, :least]
    if not even:

        @pl.when(branch == wide)
        def _():
            right_all[me, least:] = right_send[wide, least:]

    if redo:

        @pl.when(dap == 0)
        def _():
            left_last[me] = left_send[end]

    for k in (8, 9, 10, 11, 12, 13, 14):
        loads[k].wait()
    chip_pairs = nb * pairs
    lane_pair = iota((1, chip_pairs), 1)
    key_pair = lane_keys(chip_pairs)
    residue = (lane_pair // pairs * nz + dap) * rows + lax.rem(lane_pair // amino, rows)
    ilane = dot(aflag, (iota((amino, chip_pairs), 0) == residue).astype(BF16))[0:1, :]
    key_pair = jnp.where(ilane > 0.5, key_pair, 0.0).astype(jnp.int32)
    slot = iota((slots, 1), 0)
    gather = jnp.where(
        (key_pair == side * part + slot // block_rows + 1) & (lane_pair // amino == lax.rem(slot, block_rows)),
        1.0,
        0.0,
    ).astype(BF16)
    eye = iota((amino, amino), 0) == iota((amino, amino), 1)
    wide_key = jnp.broadcast_to(lane_keys(amino), (amino, amino))
    key_col = jnp.sum(jnp.where(eye, wide_key, 0.0), axis=1, keepdims=True).astype(jnp.int32)
    key_col = jnp.concatenate([key_col] * rows, axis=0)
    col = iota((1, nb * slots), 1)
    expand = jnp.where(
        (key_col == (nb - 1 - col // slots) * part + lax.rem(col, slots) // block_rows + 1)
        & (iota((pairs, 1), 0) // amino + branch * rows == lax.rem(col, block_rows)),
        1.0,
        0.0,
    ).astype(BF16)
    expand = jnp.concatenate([expand, expand], axis=1)
    arrived(class_all.at[other], pair_rsem.at[0])
    arrived(couple_all.at[other], pair_rsem.at[1])
    bins = embed_ref.shape[0]
    hot = []
    for b in range(nb):
        for i in range(rows):
            column = jnp.sum(
                jnp.where(eye, class_all[b, i : i + 1, :], 0).astype(F32), axis=1, keepdims=True
            ).astype(jnp.int32)
            hot.append(jnp.where(column == iota((amino, bins), 1), 1.0, 0.0))
    onehot = jnp.concatenate(hot, axis=0).astype(BF16)
    couple = couple_all[...].reshape(chip_pairs, width)
    base_buf[...] = (couple.astype(F32) + dot(onehot, embed_ref[...])).reshape(nb, pairs, width)
    base_c = dot(gather, couple) + dot(dot(gather, onehot).astype(BF16), embed_ref[...])

    if redo:

        @pl.when(dap == end)
        def _():
            base_send[...] = base_c.astype(BF16)

        push(base_send, base_last, base_sems.at[0], base_sems.at[1], (branch, 0), dap == end)

    for z in chips:
        d = branch * nz + z
        arrived(left_all.at[d], left_rsem.at[z])
        push(left_all.at[d], left_all.at[d], pass_sems.at[0], pass_sems.at[1], partner)
    if redo:
        arrived(left_last.at[: nz - 1], last_sems.at[1], dap == 0)
        lasts = left_last.at[pl.ds(branch * nz, nz)]
        push(lasts, lasts, last_sems.at[2], last_sems.at[3], partner, dap == 0)
    if even:
        arrived(right_all.at[: n - 1], right_sems.at[1])
    else:
        arrived(right_all.at[: n - 1], right_sems.at[1], branch == wide)
        arrived(right_all.at[: n - 1, :least], right_sems.at[1], branch != wide)
    arrived(left_all.at[:nz], pass_sems.at[1])
    arrived(flag_all.at[: n - 1], flag_sems.at[1])

    number = jnp.maximum(jnp.sum(flag_all[...], axis=0), 1.0)
    right = jnp.concatenate([right_all[:, t].reshape(n * seqs, LANES) for t in range(groups)], axis=1)
    lane = iota((1, LANES), 1)

    def middle(left_ref, base):
        left = jnp.concatenate([left_ref[:, b].reshape(n * seqs, LANES) for b in range(nb)], axis=1)
        outer = lax.dot_general(left, right, (((0,), (0,)), ((), ())), preferred_element_type=F32)
        for t in range(groups):
            for i in range(block_rows):
                outer_buf[t, pl.ds(i * (inner + 1), inner), :] = outer[
                    i * inner : (i + 1) * inner, t * LANES : (t + 1) * LANES
                ]
        parts = [[] for _ in range(part)]
        for t in range(groups):
            for q in range(inner // reps):
                block = [outer_buf[t, pl.ds(q * reps + g, block_rows, stride=inner + 1), :] for g in range(reps)]
                span = reps // 2
                while span:
                    upper = (lane // (span * inner)) % 2 == 1
                    new = list(block)
                    for a in range(reps):
                        if a & span:
                            continue
                        b = a | span
                        shift = span * inner
                        new[a] = jnp.where(upper, pltpu.roll(block[b], shift, 1), block[a])
                        new[b] = jnp.where(upper, block[b], pltpu.roll(block[a], LANES - shift, 1))
                    block = new
                    span //= 2
                for g in range(reps):
                    parts[t * reps + g].append(block[g])
        packed = jnp.concatenate([jnp.concatenate(p, axis=1) for p in parts], axis=0).astype(BF16)
        product = dot(packed, wout_ref[...]) / number
        pair_c = standardize(base + product, cgain_ref[...]).astype(BF16)
        right_two = dot(pair_c, wedge_ref[:, 2 * width :])
        tri_right = jax.nn.sigmoid(right_two[:, :width]) * right_two[:, width:]
        return product, pair_c, tri_right.astype(BF16)

    product, pair_c, tri_all[dap] = middle(left_all, base_c)
    full = None if even else branch == wide
    short = None if even else branch != wide

    def tri_block(z, size):
        return tri_all.at[z, :size]

    for z in chips:
        skip = redo & (dap == end) & (z == 0)
        if even:
            push(tri_all.at[dap], tri_all.at[dap], tri_ssem.at[0], tri_rsem.at[dap], (branch, z), ~skip)
        else:
            for size, when in ((slots, full), (firm, short)):
                push(
                    tri_block(dap, size), tri_block(dap, size), tri_ssem.at[0], tri_rsem.at[dap], (branch, z),
                    when & ~skip,
                )

    product_all[branch] = product
    share(product_all, 2)
    left_two = dot(pair_c, wedge_ref[:, : 2 * width])
    edge_buf[...] = (jax.nn.sigmoid(left_two[:, :width]) * left_two[:, width:]).astype(BF16).astype(F32)
    for i in range(block_rows):
        for k in range(part):
            row = edge_buf[k * block_rows + i : k * block_rows + i + 1, :]
            spread_buf[i, k * SUB : (k + 1) * SUB, :] = jnp.broadcast_to(row, (SUB, width))

    def triangle(z, side, store):
        block = tri_all[z].astype(F32)
        for i in range(rows):
            both = spread_buf[side * rows + i] * block
            store[z, i] = jnp.sum(both.reshape(part, SUB, width), axis=0)

    def contribute(z):
        triangle(z, other, part_send)
        push(part_send.at[z], part_in.at[z], part_ssem.at[0], part_rsem.at[0], partner)
        triangle(z, branch, own_buf)

    def settle(z):
        for i in range(rows):
            total = own_buf[z, i] + part_in[z, i]
            for b in range(nb):
                row = i * amino + (b * nz + z) * rows
                tri_buf[pl.ds(pl.multiple_of(row, rows), rows), :] = total[b * rows : (b + 1) * rows]

    contribute(dap)
    if redo:

        @pl.when(dap == 0)
        def _():
            arrived(left_last.at[:nz], last_sems.at[3])
            arrived(base_last, base_sems.at[1])
            tri_all[end] = middle(left_last, base_last[...].astype(F32))[2]
            contribute(end)

    def refresh():
        arrived(product_all.at[other], pair_rsem.at[2])
        whole = product_all[...].reshape(nb * slots, width)
        high = whole.astype(BF16)
        rest = (whole - high.astype(F32)).astype(BF16)
        updated = base_buf[branch] + dot(expand, jnp.concatenate([high, rest], axis=0))
        pair = standardize(updated, cgain_ref[...]).astype(BF16)
        updated_buf[...] = updated
        gate_buf[...] = jax.nn.sigmoid(dot(pair, wgate_ref[...]))

    pl.when(dap != 0)(refresh)
    late = [jnp.where(dap == 0, k + 1, (k + 1 + (k + 1 >= dap)) % nz) for k in range(nz - 1)]
    late = [jnp.where((dap == 0) | (k < nz - 2), z, 0) for k, z in enumerate(late)]
    for k, z in enumerate(late):
        skip = redo & (dap == 0) & (z == end)

        @pl.when(~skip)
        def _():
            if even:
                arrived(tri_all.at[z], tri_rsem.at[z])
            else:
                arrived(tri_block(z, slots), tri_rsem.at[z], full)
                arrived(tri_block(z, firm), tri_rsem.at[z], short)
            contribute(z)
    pl.when(dap == 0)(refresh)
    arrived(part_in, part_rsem.at[0])
    for z in range(nz):
        settle(z)
    tri = standardize(tri_buf[...], tgain_ref[...]).astype(BF16)
    out_ref[...] = (updated_buf[...] + gate_buf[...] * dot(tri, wfin_ref[...])).astype(BF16)
    for b in range(nb):
        size = most if even or b == wide else least
        drain(right_all.at[: nz - 1, :size], right_sems.at[0])
        drain(right_all.at[:1, :size], right_sems.at[0], branch != b)
    drain(left_all.at[: n - 1], pass_sems.at[0])
    drain(flag_all.at[: n - 1], flag_sems.at[0])
    if redo:
        drain(left_last.at[0], last_sems.at[0], dap != 0)
        drain(left_last.at[:nz], last_sems.at[2], dap == 0)
        drain(base_send, base_sems.at[0], dap == end)
    for fewer, last in ((1, redo & (dap == end)), (0, ~(redo & (dap == end)))):
        if even:
            drain(tri_all.at[: nz - 1 - fewer], tri_ssem.at[0], last)
        else:
            drain(tri_all.at[: nz - 1 - fewer], tri_ssem.at[0], last & full)
            drain(tri_all.at[: nz - 1 - fewer, :firm], tri_ssem.at[0], last & short)
    drain(part_send, part_ssem.at[0])
    for k, ref in enumerate((class_all, couple_all, product_all)):
        drain(ref.at[branch], pair_ssem.at[k])


def on_device(nb, nz, x, hflags, aflags, classes, couple, hgain, wl, wr, wout, embed, cgain, wedge, wgate, wfin, tgain):
    n = nb * nz
    seqs, amino, depth = x.shape
    rows, _, width = couple.shape
    inner = wl.shape[1]
    live = amino - 3 * amino // 8
    groups = -(-(live // (LANES // inner)) // nb)
    part = groups * (LANES // inner)
    slots = part * nb * rows
    dma = pltpu.SemaphoreType.DMA
    operands = (
        x.reshape(seqs * amino, depth), hflags.reshape(1, seqs), aflags.reshape(1, amino), classes,
        couple.reshape(rows * amino, width), hgain.reshape(1, depth), wl.T, wr.T, wout, embed,
        cgain.reshape(1, width), wedge, wgate, wfin, tgain.reshape(1, width),
    )
    held = [pltpu.VMEM((nb, *a.shape) if k in (3, 4) else a.shape, a.dtype) for k, a in enumerate(operands)]
    out = pl.pallas_call(
        functools.partial(kernel, nb, nz),
        out_shape=pltpu.VMEM((rows * amino, width), BF16),
        in_specs=[pl.BlockSpec(memory_space=pl.ANY)] * OPERANDS,
        out_specs=pl.BlockSpec(memory_space=pltpu.VMEM),
        scratch_shapes=held
        + [
            dma((OPERANDS,)),
            pltpu.VMEM((n, 1, LANES), F32),
            pltpu.VMEM((nb, groups, seqs, LANES), BF16),
            pltpu.VMEM((n, groups, seqs, LANES), BF16),
            pltpu.VMEM((nz, nb, seqs, LANES), BF16),
            pltpu.VMEM((n, nb, seqs, LANES), BF16),
            pltpu.VMEM((n, nb, seqs, LANES), BF16),
            pltpu.VMEM((nz, slots, width), BF16),
            pltpu.VMEM((seqs * (amino + 1), LANES), F32),
            pltpu.VMEM((groups, nb * rows * (inner + 1), LANES), F32),
            pltpu.VMEM((nb, rows * amino, width), F32),
            pltpu.VMEM((slots, width), BF16),
            pltpu.VMEM((slots, width), BF16),
            pltpu.VMEM((nb, slots, width), F32),
            pltpu.VMEM((slots, width), F32),
            pltpu.VMEM((nb * rows, slots, width), F32),
            pltpu.VMEM((nz, rows, SUB, width), F32),
            pltpu.VMEM((nz, rows, SUB, width), F32),
            pltpu.VMEM((nz, rows, SUB, width), F32),
            pltpu.VMEM((rows * amino, width), F32),
            pltpu.VMEM((rows * amino, width), F32),
            pltpu.VMEM((rows * amino, width), F32),
        ]
        + [dma((2,)), dma((2,)), dma((2,)), dma((4,)), dma((2,)), dma((nz,))]
        + [dma((1,)), dma((nz,)), dma((1,)), dma((1,)), dma((3,)), dma((3,))]
        + [pltpu.SemaphoreType.REGULAR((nz - 1,))],
        compiler_params=pltpu.CompilerParams(collective_id=0, has_side_effects=True),
    )(*operands)
    return out.reshape(rows, amino, width)


def solution(mesh):
    split = ("rep", "branch", "dap")
    placed = (
        P(split, None, None), P(split), P("rep"), P(split, None), P(split, None, None),
        P(), P(), P(), P(), P(), P(), P(), P(), P(), P(),
    )
    return jax.shard_map(
        functools.partial(on_device, mesh.shape["branch"], mesh.shape["dap"]),
        mesh=mesh,
        in_specs=placed,
        out_specs=P(split, None, None),
        check_vma=False,
    )
```

```python
import functools

import jax
import jax.numpy as jnp
from jax import lax
from jax.experimental import pallas as pl
from jax.experimental.pallas import tpu as pltpu
from jax.sharding import PartitionSpec as P

F32 = jnp.float32
BF16 = jnp.bfloat16
MESH = pl.DeviceIdType.MESH
OPERANDS = 15
LANES = 128
SUB = 8


def iota(shape, axis):
    return lax.broadcasted_iota(jnp.int32, shape, axis)


def dot(a, b):
    return jnp.dot(a, b, preferred_element_type=F32)


def standardize(values, gain):
    mean = jnp.mean(values, axis=-1, keepdims=True)
    centred = values - mean
    spread = jnp.mean(centred * centred, axis=-1, keepdims=True)
    return centred * lax.rsqrt(spread + 1e-05) * gain


def kernel(
    nb, nz,
    *refs,
):
    operands, out_ref, held = refs[:OPERANDS], refs[OPERANDS], refs[OPERANDS + 1 : 2 * OPERANDS + 1]
    in_sem, *scratch = refs[2 * OPERANDS + 1 :]
    (x_ref, hflag_ref, aflag_ref, class_all, couple_all, hgain_ref, wl_ref, wr_ref, wout_ref,
     embed_ref, cgain_ref, wedge_ref, wgate_ref, wfin_ref, tgain_ref) = held
    (
    flag_all, right_send, right_all, left_send, left_all, left_last, tri_all, y_left, outer_buf,
    base_buf, base_send, base_last, product_all, edge_buf, spread_buf, own_buf, part_send, part_in, tri_buf, updated_buf, gate_buf,
    flag_sems, right_sems, pass_sems, last_sems, base_sems, left_rsem, tri_ssem, tri_rsem, part_ssem, part_rsem,
    pair_ssem, pair_rsem, ready,
    ) = scratch
    n = nb * nz
    branch = lax.axis_index("branch")
    dap = lax.axis_index("dap")
    me = branch * nz + dap
    amino = aflag_ref.shape[1]
    seqs = hflag_ref.shape[1]
    rows = class_all.shape[1]
    inner = wl_ref.shape[0]
    width = couple_all.shape[2]
    reps = LANES // inner
    live = amino - 3 * amino // 8
    tiles = live // reps
    groups = -(-tiles // nb)
    even = tiles % nb == 0
    part = groups * reps
    most = groups
    least = most if even else most - 1
    block_rows = nb * rows
    slots = part * block_rows
    firm = slots - reps * block_rows
    pairs = rows * amino
    side = nb - 1 - branch
    wide = nb - 1
    chips = [k + (k >= dap) for k in range(nz - 1)]
    redo = nz > 2
    end = nz - 1
    order = []
    for k in range(nz - 1):
        rank = jnp.where(dap == 0, nz - 2, jnp.where(dap == end, end, dap - 1))
        rank = k + (k >= rank)
        order.append(jnp.where(rank < nz - 2, rank + 1, jnp.where(rank == nz - 2, 0, end)))
    other = nb - 1 - branch
    partner = (other, dap)
    everyone = [partner] + [(b, z) for z in chips for b in (branch, other)]

    def index_of(peer):
        return peer[0] * nz + peer[1]

    def target(peer):
        return {"branch": peer[0], "dap": peer[1]}

    loads = {}
    for k in (2,1,0,5,6,7,8,3,4,9,10,11,12,13,14):
        place = held[k].at[branch] if k in (3, 4) else held[k]
        loads[k] = pltpu.make_async_copy(operands[k], place, in_sem.at[k])
        if k == 0:
            step = x_ref.shape[0] // 8
            for j in range(8):
                piece = pl.ds(j * step, step)
                pltpu.make_async_copy(operands[0].at[piece], x_ref.at[piece], in_sem.at[0]).start()
        else:
            loads[k].start()

    barrier = pltpu.get_barrier_semaphore()
    pl.semaphore_signal(barrier, inc=1, device_id=target(partner), device_id_type=MESH)
    for b, z in everyone[1:]:

        @pl.when(z > dap)
        def _():
            pl.semaphore_signal(barrier, inc=1, device_id=target((b, z)), device_id_type=MESH)

    pl.semaphore_wait(barrier, dap * nb + 1)
    for b, z in everyone[1:]:

        @pl.when(z < dap)
        def _():
            pl.semaphore_signal(ready.at[dap - 1], inc=1, device_id=target((b, z)), device_id_type=MESH)

    if not even:

        @pl.when(branch != wide)
        def _():
            right_all[:, least:] = jnp.zeros((n, most - least, seqs, LANES), BF16)
            tri_all[:, firm:, :] = jnp.zeros((nz, slots - firm, width), BF16)

    loads[2].wait()
    loads[1].wait()
    aflag = jnp.broadcast_to(aflag_ref[...].astype(F32), (SUB, amino)).astype(BF16)
    hflag32 = hflag_ref[...].astype(F32)
    hflag = jnp.broadcast_to(hflag32, (SUB, seqs)).astype(BF16)

    def lane_keys(lanes):
        r = iota((amino, lanes), 0)
        k = lax.rem(iota((amino, lanes), 1), amino)
        count = dot(aflag, (r <= k).astype(BF16))
        alive = dot(aflag, (r == k).astype(BF16))
        return (count * alive)[0:1, :]

    flag_all[me] = jnp.broadcast_to(jnp.sum(hflag32, axis=1, keepdims=True), (1, LANES))

    total = seqs * amino
    span = SUB * amino
    key_x = lane_keys(span)
    hlane = dot(hflag, (iota((seqs, total), 0) == iota((seqs, total), 1) // amino).astype(BF16))[0:1, :]
    gather_right = []
    for h in range(seqs // SUB):
        code = (key_x - 1.0) * SUB + (iota((1, span), 1) // amino).astype(F32)
        code = jnp.where(hlane[:, h * span : (h + 1) * span] * key_x > 0.5, code, -1.0).astype(jnp.int32)
        gather_right.append(jnp.where(iota((live * SUB, 1), 0) == code, 1.0, 0.0).astype(BF16))
    lane_group = iota((1, LANES), 1) // inner
    alane = dot(
        aflag,
        (iota((amino, amino * inner), 0) == iota((amino, amino * inner), 1) // inner).astype(BF16),
    )[0:1, :]

    for k in (0, 5, 6, 7):
        loads[k].wait()
    depth = x_ref.shape[1]
    mean = dot(x_ref[...], jnp.ones((depth, LANES), BF16)) * (1.0 / depth)
    centred = x_ref[...].astype(F32) - jnp.concatenate([mean] * (depth // LANES), axis=1)
    spread = jnp.mean(centred * centred, axis=-1, keepdims=True)
    normed = (centred * lax.rsqrt(spread + 1e-05) * hgain_ref[...]).astype(BF16)
    w_both = jnp.concatenate([wl_ref[...]] * reps + [wr_ref[...]] * reps, axis=0)
    sides = lax.dot_general(
        normed, w_both, (((1,), (1,)), ((), ())), preferred_element_type=F32
    )
    for i in range(seqs):
        y_left[pl.ds(i * (amino + 1), amino), :] = sides[i * amino : (i + 1) * amino, :LANES]
    for d in range(n):
        block = y_left[pl.ds(d * rows, seqs, stride=amino + 1), :]
        for g in range(1, rows):
            block = jnp.where(
                lane_group == g, y_left[pl.ds(d * rows + g, seqs, stride=amino + 1), :], block
            )
        left_send[d % nz, d // nz] = (block * alane[:, d * LANES : (d + 1) * LANES]).astype(BF16)

    def guarded(when, act):
        if when is None:
            act()
        else:
            pl.when(when)(act)

    def push(src, dst, ssem, rsem, peer, when=None):
        copy = pltpu.make_async_remote_copy(
            src_ref=src, dst_ref=dst, send_sem=ssem, recv_sem=rsem,
            device_id=target(peer), device_id_type=MESH,
        )
        guarded(when, copy.start)

    def push_left(z):
        push(left_send.at[z], left_all.at[me], pass_sems.at[0], left_rsem.at[dap], (branch, z))

    first_left = order[:1]
    for z in first_left:
        pl.when(z < dap)(functools.partial(push_left, z))
    right_rows = [
        dot(gather, sides[h * span : (h + 1) * span, LANES:].astype(BF16)) for h, gather in enumerate(gather_right)
    ]

    def right_of(k):
        return jnp.concatenate([part_rows[k * SUB : (k + 1) * SUB] for part_rows in right_rows], axis=0)

    for b in range(nb):
        for t in range(min(groups, tiles - (nb - 1 - b) * groups)):
            begin = (nb - 1 - b) * part + t * reps
            block = right_of(begin)
            for g in range(1, reps):
                block = jnp.where(lane_group == g, right_of(begin + g), block)
            right_send[b, t] = block.astype(BF16)

    def drain(ref, ssem, when=None):
        wait = pltpu.make_async_remote_copy(
            src_ref=ref, dst_ref=ref, send_sem=ssem, recv_sem=ssem,
            device_id=target(partner), device_id_type=MESH,
        ).wait_send
        guarded(when, wait)

    def arrived(ref, rsem, when=None):
        wait = pltpu.make_async_remote_copy(
            src_ref=ref, dst_ref=ref, send_sem=rsem,
            recv_sem=rsem, device_id=target(partner), device_id_type=MESH,
        ).wait_recv
        guarded(when, wait)

    def share(ref, k):
        push(ref.at[branch], ref.at[branch], pair_ssem.at[k], pair_rsem.at[k], partner)

    def push_right(b, z, when=None):
        size = most if even or b == wide else least
        push(
            right_send.at[b, :size], right_all.at[me, :size], right_sems.at[0], right_sems.at[1], (b, z), when
        )

    for k, z in enumerate(order):

        @pl.when(z > dap)
        def _():
            pl.semaphore_wait(ready.at[z - 1], nb)

        if k < len(first_left):
            pl.when(z > dap)(functools.partial(push_left, z))
        else:
            push_left(z)
        if redo:
            push(left_send.at[end], left_last.at[me], last_sems.at[0], last_sems.at[1], (branch, 0), z == 0)
        for b in range(nb):
            push_right(b, z)
        for b in range(nb):
            push(flag_all.at[me], flag_all.at[me], flag_sems.at[0], flag_sems.at[1], (b, z))
    for b in range(nb):
        push_right(b, dap, branch != b)
    push(left_send.at[dap], left_all.at[me], pass_sems.at[0], pass_sems.at[1], partner)
    push(flag_all.at[me], flag_all.at[me], flag_sems.at[0], flag_sems.at[1], partner)
    for k in (3, 4):
        loads[k].wait()
    share(class_all, 0)
    share(couple_all, 1)
    left_all[me] = left_send[dap]
    right_all[me, :least] = right_send[branch, :least]
    if not even:

        @pl.when(branch == wide)
        def _():
            right_all[me, least:] = right_send[wide, least:]

    if redo:

        @pl.when(dap == 0)
        def _():
            left_last[me] = left_send[end]

    for k in (8, 9, 10, 11, 12, 13, 14):
        loads[k].wait()
    chip_pairs = nb * pairs
    lane_pair = iota((1, chip_pairs), 1)
    key_pair = lane_keys(chip_pairs)
    residue = (lane_pair // pairs * nz + dap) * rows + lax.rem(lane_pair // amino, rows)
    ilane = dot(aflag, (iota((amino, chip_pairs), 0) == residue).astype(BF16))[0:1, :]
    key_pair = jnp.where(ilane > 0.5, key_pair, 0.0).astype(jnp.int32)
    slot = iota((slots, 1), 0)
    gather = jnp.where(
        (key_pair == side * part + slot // block_rows + 1) & (lane_pair // amino == lax.rem(slot, block_rows)),
        1.0,
        0.0,
    ).astype(BF16)
    eye = iota((amino, amino), 0) == iota((amino, amino), 1)
    wide_key = jnp.broadcast_to(lane_keys(amino), (amino, amino))
    key_col = jnp.sum(jnp.where(eye, wide_key, 0.0), axis=1, keepdims=True).astype(jnp.int32)
    key_col = jnp.concatenate([key_col] * rows, axis=0)
    col = iota((1, nb * slots), 1)
    expand = jnp.where(
        (key_col == (nb - 1 - col // slots) * part + lax.rem(col, slots) // block_rows + 1)
        & (iota((pairs, 1), 0) // amino + branch * rows == lax.rem(col, block_rows)),
        1.0,
        0.0,
    ).astype(BF16)
    expand = jnp.concatenate([expand, expand], axis=1)
    arrived(class_all.at[other], pair_rsem.at[0])
    arrived(couple_all.at[other], pair_rsem.at[1])
    bins = embed_ref.shape[0]
    hot = []
    for b in range(nb):
        for i in range(rows):
            column = jnp.sum(
                jnp.where(eye, class_all[b, i : i + 1, :], 0).astype(F32), axis=1, keepdims=True
            ).astype(jnp.int32)
            hot.append(jnp.where(column == iota((amino, bins), 1), 1.0, 0.0))
    onehot = jnp.concatenate(hot, axis=0).astype(BF16)
    couple = couple_all[...].reshape(chip_pairs, width)
    base_buf[...] = (couple.astype(F32) + dot(onehot, embed_ref[...])).reshape(nb, pairs, width)
    base_c = dot(gather, couple) + dot(dot(gather, onehot).astype(BF16), embed_ref[...])

    if redo:

        @pl.when(dap == end)
        def _():
            base_send[...] = base_c.astype(BF16)

        push(base_send, base_last, base_sems.at[0], base_sems.at[1], (branch, 0), dap == end)

    for z in chips:
        d = branch * nz + z
        arrived(left_all.at[d], left_rsem.at[z])
        push(left_all.at[d], left_all.at[d], pass_sems.at[0], pass_sems.at[1], partner)
    if redo:
        arrived(left_last.at[: nz - 1], last_sems.at[1], dap == 0)
        lasts = left_last.at[pl.ds(branch * nz, nz)]
        push(lasts, lasts, last_sems.at[2], last_sems.at[3], partner, dap == 0)
    if even:
        arrived(right_all.at[: n - 1], right_sems.at[1])
    else:
        arrived(right_all.at[: n - 1], right_sems.at[1], branch == wide)
        arrived(right_all.at[: n - 1, :least], right_sems.at[1], branch != wide)
    arrived(left_all.at[:nz], pass_sems.at[1])
    arrived(flag_all.at[: n - 1], flag_sems.at[1])

    number = jnp.maximum(jnp.sum(flag_all[...], axis=0), 1.0)
    right = jnp.concatenate([right_all[:, t].reshape(n * seqs, LANES) for t in range(groups)], axis=1)
    lane = iota((1, LANES), 1)

    def middle(left_ref, base):
        left = jnp.concatenate([left_ref[:, b].reshape(n * seqs, LANES) for b in range(nb)], axis=1)
        outer = lax.dot_general(left, right, (((0,), (0,)), ((), ())), preferred_element_type=F32)
        for t in range(groups):
            for i in range(block_rows):
                outer_buf[t, pl.ds(i * (inner + 1), inner), :] = outer[
                    i * inner : (i + 1) * inner, t * LANES : (t + 1) * LANES
                ]
        parts = [[] for _ in range(part)]
        for t in range(groups):
            for q in range(inner // reps):
                block = [outer_buf[t, pl.ds(q * reps + g, block_rows, stride=inner + 1), :] for g in range(reps)]
                span = reps // 2
                while span:
                    upper = (lane // (span * inner)) % 2 == 1
                    new = list(block)
                    for a in range(reps):
                        if a & span:
                            continue
                        b = a | span
                        shift = span * inner
                        new[a] = jnp.where(upper, pltpu.roll(block[b], shift, 1), block[a])
                        new[b] = jnp.where(upper, block[b], pltpu.roll(block[a], LANES - shift, 1))
                    block = new
                    span //= 2
                for g in range(reps):
                    parts[t * reps + g].append(block[g])
        packed = jnp.concatenate([jnp.concatenate(p, axis=1) for p in parts], axis=0).astype(BF16)
        product = dot(packed, wout_ref[...]) / number
        pair_c = standardize(base + product, cgain_ref[...]).astype(BF16)
        right_two = dot(pair_c, wedge_ref[:, 2 * width :])
        tri_right = jax.nn.sigmoid(right_two[:, :width]) * right_two[:, width:]
        return product, pair_c, tri_right.astype(BF16)

    product, pair_c, tri_all[dap] = middle(left_all, base_c)
    full = None if even else branch == wide
    short = None if even else branch != wide

    def tri_block(z, size):
        return tri_all.at[z, :size]

    for z in chips:
        skip = redo & (dap == end) & (z == 0)
        if even:
            push(tri_all.at[dap], tri_all.at[dap], tri_ssem.at[0], tri_rsem.at[dap], (branch, z), ~skip)
        else:
            for size, when in ((slots, full), (firm, short)):
                push(
                    tri_block(dap, size), tri_block(dap, size), tri_ssem.at[0], tri_rsem.at[dap], (branch, z),
                    when & ~skip,
                )

    product_all[branch] = product
    share(product_all, 2)
    left_two = dot(pair_c, wedge_ref[:, : 2 * width])
    edge_buf[...] = (jax.nn.sigmoid(left_two[:, :width]) * left_two[:, width:]).astype(BF16).astype(F32)
    for i in range(block_rows):
        for k in range(part):
            row = edge_buf[k * block_rows + i : k * block_rows + i + 1, :]
            spread_buf[i, k * SUB : (k + 1) * SUB, :] = jnp.broadcast_to(row, (SUB, width))

    def triangle(z, side, store):
        block = tri_all[z].astype(F32)
        for i in range(rows):
            both = spread_buf[side * rows + i] * block
            store[z, i] = jnp.sum(both.reshape(part, SUB, width), axis=0)

    def contribute(z):
        triangle(z, other, part_send)
        push(part_send.at[z], part_in.at[z], part_ssem.at[0], part_rsem.at[0], partner)
        triangle(z, branch, own_buf)

    def settle(z):
        for i in range(rows):
            total = own_buf[z, i] + part_in[z, i]
            for b in range(nb):
                row = i * amino + (b * nz + z) * rows
                tri_buf[pl.ds(pl.multiple_of(row, rows), rows), :] = total[b * rows : (b + 1) * rows]

    contribute(dap)
    if redo:

        @pl.when(dap == 0)
        def _():
            arrived(left_last.at[:nz], last_sems.at[3])
            arrived(base_last, base_sems.at[1])
            tri_all[end] = middle(left_last, base_last[...].astype(F32))[2]
            contribute(end)

    def refresh():
        arrived(product_all.at[other], pair_rsem.at[2])
        whole = product_all[...].reshape(nb * slots, width)
        high = whole.astype(BF16)
        rest = (whole - high.astype(F32)).astype(BF16)
        updated = base_buf[branch] + dot(expand, jnp.concatenate([high, rest], axis=0))
        pair = standardize(updated, cgain_ref[...]).astype(BF16)
        updated_buf[...] = updated
        gate_buf[...] = jax.nn.sigmoid(dot(pair, wgate_ref[...]))

    pl.when(dap != 0)(refresh)
    late = [jnp.where(dap == 0, k + 1, (k + 1 + (k + 1 >= dap)) % nz) for k in range(nz - 1)]
    late = [jnp.where((dap == 0) | (k < nz - 2), z, 0) for k, z in enumerate(late)]
    for k, z in enumerate(late):
        skip = redo & (dap == 0) & (z == end)

        @pl.when(~skip)
        def _():
            if even:
                arrived(tri_all.at[z], tri_rsem.at[z])
            else:
                arrived(tri_block(z, slots), tri_rsem.at[z], full)
                arrived(tri_block(z, firm), tri_rsem.at[z], short)
            contribute(z)
    pl.when(dap == 0)(refresh)
    arrived(part_in, part_rsem.at[0])
    for z in range(nz):
        settle(z)
    tri = standardize(tri_buf[...], tgain_ref[...]).astype(BF16)
    out_ref[...] = (updated_buf[...] + gate_buf[...] * dot(tri, wfin_ref[...])).astype(BF16)
    for b in range(nb):
        size = most if even or b == wide else least
        drain(right_all.at[: nz - 1, :size], right_sems.at[0])
        drain(right_all.at[:1, :size], right_sems.at[0], branch != b)
    drain(left_all.at[: n - 1], pass_sems.at[0])
    drain(flag_all.at[: n - 1], flag_sems.at[0])
    if redo:
        drain(left_last.at[0], last_sems.at[0], dap != 0)
        drain(left_last.at[:nz], last_sems.at[2], dap == 0)
        drain(base_send, base_sems.at[0], dap == end)
    for fewer, last in ((1, redo & (dap == end)), (0, ~(redo & (dap == end)))):
        if even:
            drain(tri_all.at[: nz - 1 - fewer], tri_ssem.at[0], last)
        else:
            drain(tri_all.at[: nz - 1 - fewer], tri_ssem.at[0], last & full)
            drain(tri_all.at[: nz - 1 - fewer, :firm], tri_ssem.at[0], last & short)
    drain(part_send, part_ssem.at[0])
    for k, ref in enumerate((class_all, couple_all, product_all)):
        drain(ref.at[branch], pair_ssem.at[k])


def on_device(nb, nz, x, hflags, aflags, classes, couple, hgain, wl, wr, wout, embed, cgain, wedge, wgate, wfin, tgain):
    n = nb * nz
    seqs, amino, depth = x.shape
    rows, _, width = couple.shape
    inner = wl.shape[1]
    live = amino - 3 * amino // 8
    groups = -(-(live // (LANES // inner)) // nb)
    part = groups * (LANES // inner)
    slots = part * nb * rows
    dma = pltpu.SemaphoreType.DMA
    operands = (
        x.reshape(seqs * amino, depth), hflags.reshape(1, seqs), aflags.reshape(1, amino), classes,
        couple.reshape(rows * amino, width), hgain.reshape(1, depth), wl.T, wr.T, wout, embed,
        cgain.reshape(1, width), wedge, wgate, wfin, tgain.reshape(1, width),
    )
    held = [pltpu.VMEM((nb, *a.shape) if k in (3, 4) else a.shape, a.dtype) for k, a in enumerate(operands)]
    out = pl.pallas_call(
        functools.partial(kernel, nb, nz),
        out_shape=pltpu.VMEM((rows * amino, width), BF16),
        in_specs=[pl.BlockSpec(memory_space=pl.ANY)] * OPERANDS,
        out_specs=pl.BlockSpec(memory_space=pltpu.VMEM),
        scratch_shapes=held
        + [
            dma((OPERANDS,)),
            pltpu.VMEM((n, 1, LANES), F32),
            pltpu.VMEM((nb, groups, seqs, LANES), BF16),
            pltpu.VMEM((n, groups, seqs, LANES), BF16),
            pltpu.VMEM((nz, nb, seqs, LANES), BF16),
            pltpu.VMEM((n, nb, seqs, LANES), BF16),
            pltpu.VMEM((n, nb, seqs, LANES), BF16),
            pltpu.VMEM((nz, slots, width), BF16),
            pltpu.VMEM((seqs * (amino + 1), LANES), F32),
            pltpu.VMEM((groups, nb * rows * (inner + 1), LANES), F32),
            pltpu.VMEM((nb, rows * amino, width), F32),
            pltpu.VMEM((slots, width), BF16),
            pltpu.VMEM((slots, width), BF16),
            pltpu.VMEM((nb, slots, width), F32),
            pltpu.VMEM((slots, width), F32),
            pltpu.VMEM((nb * rows, slots, width), F32),
            pltpu.VMEM((nz, rows, SUB, width), F32),
            pltpu.VMEM((nz, rows, SUB, width), F32),
            pltpu.VMEM((nz, rows, SUB, width), F32),
            pltpu.VMEM((rows * amino, width), F32),
            pltpu.VMEM((rows * amino, width), F32),
            pltpu.VMEM((rows * amino, width), F32),
        ]
        + [dma((2,)), dma((2,)), dma((2,)), dma((4,)), dma((2,)), dma((nz,))]
        + [dma((1,)), dma((nz,)), dma((1,)), dma((1,)), dma((3,)), dma((3,))]
        + [pltpu.SemaphoreType.REGULAR((nz - 1,))],
        compiler_params=pltpu.CompilerParams(collective_id=0, has_side_effects=True),
    )(*operands)
    return out.reshape(rows, amino, width)


def solution(mesh):
    split = ("rep", "branch", "dap")
    placed = (
        P(split, None, None), P(split), P("rep"), P(split, None), P(split, None, None),
        P(), P(), P(), P(), P(), P(), P(), P(), P(), P(),
    )
    return jax.shard_map(
        functools.partial(on_device, mesh.shape["branch"], mesh.shape["dap"]),
        mesh=mesh,
        in_specs=placed,
        out_specs=P(split, None, None),
        check_vma=False,
    )
```

```python
import functools

import jax
import jax.numpy as jnp
from jax import lax
from jax.experimental import pallas as pl
from jax.experimental.pallas import tpu as pltpu
from jax.sharding import PartitionSpec as P

F32 = jnp.float32
BF16 = jnp.bfloat16
MESH = pl.DeviceIdType.MESH
OPERANDS = 15
HELD = 11
LANES = 128
SUB = 8


def iota(shape, axis):
    return lax.broadcasted_iota(jnp.int32, shape, axis)


def dot(a, b):
    return jnp.dot(a, b, preferred_element_type=F32)


def standardize(values, gain):
    mean = jnp.mean(values, axis=-1, keepdims=True)
    centred = values - mean
    spread = jnp.mean(centred * centred, axis=-1, keepdims=True)
    return centred * lax.rsqrt(spread + 1e-05) * gain


def kernel(
    nb, nz,
    *refs,
):
    operands, out_ref, held = refs[:OPERANDS], refs[OPERANDS], refs[OPERANDS + 1 : OPERANDS + 1 + HELD]
    in_sem, *scratch = refs[OPERANDS + 1 + HELD :]
    x_ref, hflag_ref, aflag_ref, class_all, couple_all, hgain_ref, side_ref, tall_ref, embed_ref, gain_ref, wedge_ref = held
    (
    flag_all, right_send, right_all, left_send, left_all, left_last, tri_all, y_left, outer_buf,
    base_buf, base_send, base_last, product_all, edge_buf, spread_buf, own_buf, part_send, part_in, tri_buf, updated_buf, gate_buf,
    flag_sems, right_sems, pass_sems, last_sems, base_sems, left_rsem, tri_ssem, tri_rsem, part_ssem, part_rsem,
    pair_ssem, pair_rsem, ready,
    ) = scratch
    n = nb * nz
    branch = lax.axis_index("branch")
    dap = lax.axis_index("dap")
    me = branch * nz + dap
    amino = aflag_ref.shape[1]
    seqs = hflag_ref.shape[1]
    rows = class_all.shape[1]
    inner = side_ref.shape[1]
    width = couple_all.shape[2]
    reps = LANES // inner
    live = amino - 3 * amino // 8
    tiles = live // reps
    groups = -(-tiles // nb)
    even = tiles % nb == 0
    part = groups * reps
    most = groups
    least = most if even else most - 1
    block_rows = nb * rows
    slots = part * block_rows
    firm = slots - reps * block_rows
    pairs = rows * amino
    side = nb - 1 - branch
    wide = nb - 1
    chips = [k + (k >= dap) for k in range(nz - 1)]
    redo = nz > 2
    end = nz - 1
    order = []
    for k in range(nz - 1):
        rank = jnp.where(dap == 0, nz - 2, jnp.where(dap == end, end, dap - 1))
        rank = k + (k >= rank)
        order.append(jnp.where(rank < nz - 2, rank + 1, jnp.where(rank == nz - 2, 0, end)))
    other = nb - 1 - branch
    partner = (other, dap)
    everyone = [partner] + [(b, z) for z in chips for b in (branch, other)]

    def rank_at(z):
        return dap - (dap > z)

    def index_of(peer):
        return peer[0] * nz + peer[1]

    def target(peer):
        return {"branch": peer[0], "dap": peer[1]}

    long = inner * inner
    homes = [
        (x_ref, 0), (hflag_ref, 1), (aflag_ref, 2), (class_all.at[branch], 3), (couple_all.at[branch], 4),
        (hgain_ref, 5), (side_ref.at[0], 6), (side_ref.at[1], 6), (tall_ref.at[:long], 7), (embed_ref, 8),
        (gain_ref.at[0], 9), (wedge_ref, 10), (tall_ref.at[long : long + width], 7),
        (tall_ref.at[long + width :], 7), (gain_ref.at[1], 9),
    ]
    whole_homes = {6: side_ref, 7: tall_ref, 9: gain_ref}
    for k in (2, 1, 0, 5, 6, 7, 8, 3, 4, 9, 10, 11, 12, 13, 14):
        home, sem = homes[k]
        pieces = 8 if k == 0 else 1
        for p in range(pieces):
            step = home.shape[0] // pieces
            source, target_ref = operands[k], home
            if pieces > 1:
                source, target_ref = source.at[pl.ds(p * step, step)], target_ref.at[pl.ds(p * step, step)]
            pltpu.make_async_copy(source, target_ref, in_sem.at[sem]).start()

    def loaded(*keys):
        for sem in sorted({homes[k][1] for k in keys}):
            ref = whole_homes[sem] if sem in whole_homes else next(home for home, at in homes if at == sem)
            pltpu.make_async_copy(ref, ref, in_sem.at[sem]).wait()

    barrier = pltpu.get_barrier_semaphore()
    pl.semaphore_signal(barrier, inc=1, device_id=target(partner), device_id_type=MESH)
    for b, z in everyone[1:]:

        @pl.when(z > dap)
        def _():
            pl.semaphore_signal(barrier, inc=1, device_id=target((b, z)), device_id_type=MESH)

    pl.semaphore_wait(barrier, dap * nb + 1)
    for b, z in everyone[1:]:

        @pl.when(z < dap)
        def _():
            pl.semaphore_signal(ready.at[dap - 1], inc=1, device_id=target((b, z)), device_id_type=MESH)

    if not even:

        @pl.when(branch != wide)
        def _():
            right_all[:, least:] = jnp.zeros((n, most - least, seqs, LANES), BF16)
            tri_all[:, firm:, :] = jnp.zeros((nz, slots - firm, width), BF16)

    loaded(2, 1)
    aflag = jnp.broadcast_to(aflag_ref[...].astype(F32), (SUB, amino)).astype(BF16)
    hflag32 = hflag_ref[...].astype(F32)
    hflag = jnp.broadcast_to(hflag32, (SUB, seqs)).astype(BF16)

    def lane_keys(lanes):
        r = iota((amino, lanes), 0)
        k = lax.rem(iota((amino, lanes), 1), amino)
        count = dot(aflag, (r <= k).astype(BF16))
        alive = dot(aflag, (r == k).astype(BF16))
        return (count * alive)[0:1, :]

    flag_all[me] = jnp.broadcast_to(jnp.sum(hflag32, axis=1, keepdims=True), (1, LANES))

    total = seqs * amino
    span = SUB * amino
    key_x = lane_keys(span)
    hlane = dot(hflag, (iota((seqs, total), 0) == iota((seqs, total), 1) // amino).astype(BF16))[0:1, :]
    gather_right = []
    for h in range(seqs // SUB):
        code = (key_x - 1.0) * SUB + (iota((1, span), 1) // amino).astype(F32)
        code = jnp.where(hlane[:, h * span : (h + 1) * span] * key_x > 0.5, code, -1.0).astype(jnp.int32)
        gather_right.append(jnp.where(iota((live * SUB, 1), 0) == code, 1.0, 0.0).astype(BF16))
    lane_group = iota((1, LANES), 1) // inner
    alane = dot(
        aflag,
        (iota((amino, amino * inner), 0) == iota((amino, amino * inner), 1) // inner).astype(BF16),
    )[0:1, :]

    loaded(0, 5, 6, 7)
    depth = x_ref.shape[1]
    mean = dot(x_ref[...], jnp.ones((depth, LANES), BF16)) * (1.0 / depth)
    centred = x_ref[...].astype(F32) - jnp.concatenate([mean] * (depth // LANES), axis=1)
    spread = jnp.mean(centred * centred, axis=-1, keepdims=True)
    normed = (centred * lax.rsqrt(spread + 1e-05) * hgain_ref[...]).astype(BF16)
    w_both = jnp.concatenate([side_ref[0]] * reps + [side_ref[1]] * reps, axis=0)
    sides = lax.dot_general(
        normed, w_both, (((1,), (1,)), ((), ())), preferred_element_type=F32
    )
    for i in range(seqs):
        y_left[pl.ds(i * (amino + 1), amino), :] = sides[i * amino : (i + 1) * amino, :LANES]
    for d in range(n):
        block = y_left[pl.ds(d * rows, seqs, stride=amino + 1), :]
        for g in range(1, rows):
            block = jnp.where(
                lane_group == g, y_left[pl.ds(d * rows + g, seqs, stride=amino + 1), :], block
            )
        left_send[d % nz, d // nz] = (block * alane[:, d * LANES : (d + 1) * LANES]).astype(BF16)

    def guarded(when, act):
        if when is None:
            act()
        else:
            pl.when(when)(act)

    def push(src, dst, ssem, rsem, peer, when=None):
        copy = pltpu.make_async_remote_copy(
            src_ref=src, dst_ref=dst, send_sem=ssem, recv_sem=rsem,
            device_id=target(peer), device_id_type=MESH,
        )
        guarded(when, copy.start)

    def push_left(z):
        push(left_send.at[z], left_all.at[me], pass_sems.at[0], left_rsem.at[rank_at(z)], (branch, z))

    first_left = order[:1]
    for z in first_left:
        pl.when(z < dap)(functools.partial(push_left, z))
    right_rows = [
        dot(gather, sides[h * span : (h + 1) * span, LANES:].astype(BF16)) for h, gather in enumerate(gather_right)
    ]

    def right_of(k):
        return jnp.concatenate([part_rows[k * SUB : (k + 1) * SUB] for part_rows in right_rows], axis=0)

    for b in range(nb):
        for t in range(min(groups, tiles - (nb - 1 - b) * groups)):
            begin = (nb - 1 - b) * part + t * reps
            block = right_of(begin)
            for g in range(1, reps):
                block = jnp.where(lane_group == g, right_of(begin + g), block)
            right_send[b, t] = block.astype(BF16)

    def drain(ref, ssem, when=None):
        wait = pltpu.make_async_remote_copy(
            src_ref=ref, dst_ref=ref, send_sem=ssem, recv_sem=ssem,
            device_id=target(partner), device_id_type=MESH,
        ).wait_send
        guarded(when, wait)

    def arrived(ref, rsem, when=None):
        wait = pltpu.make_async_remote_copy(
            src_ref=ref, dst_ref=ref, send_sem=rsem,
            recv_sem=rsem, device_id=target(partner), device_id_type=MESH,
        ).wait_recv
        guarded(when, wait)

    def share(ref, k):
        push(ref.at[branch], ref.at[branch], pair_ssem.at[k], pair_rsem.at[k], partner)

    def push_right(b, z, when=None):
        size = most if even or b == wide else least
        push(
            right_send.at[b, :size], right_all.at[me, :size], right_sems.at[0], right_sems.at[1], (b, z), when
        )

    for k, z in enumerate(order):

        @pl.when(z > dap)
        def _():
            pl.semaphore_wait(ready.at[z - 1], nb)

        if k < len(first_left):
            pl.when(z > dap)(functools.partial(push_left, z))
        else:
            push_left(z)
        if redo:
            push(left_send.at[end], left_last.at[me], last_sems.at[0], last_sems.at[1], (branch, 0), z == 0)
        for b in range(nb):
            push_right(b, z)
        for b in range(nb):
            push(flag_all.at[me], flag_all.at[me], flag_sems.at[0], flag_sems.at[1], (b, z))
    for b in range(nb):
        push_right(b, dap, branch != b)
    push(left_send.at[dap], left_all.at[me], pass_sems.at[0], pass_sems.at[1], partner)
    push(flag_all.at[me], flag_all.at[me], flag_sems.at[0], flag_sems.at[1], partner)
    loaded(3, 4)
    share(class_all, 0)
    share(couple_all, 1)
    left_all[me] = left_send[dap]
    right_all[me, :least] = right_send[branch, :least]
    if not even:

        @pl.when(branch == wide)
        def _():
            right_all[me, least:] = right_send[wide, least:]

    if redo:

        @pl.when(dap == 0)
        def _():
            left_last[me] = left_send[end]

    loaded(8, 9, 10, 11)
    chip_pairs = nb * pairs
    lane_pair = iota((1, chip_pairs), 1)
    key_pair = lane_keys(chip_pairs)
    residue = (lane_pair // pairs * nz + dap) * rows + lax.rem(lane_pair // amino, rows)
    ilane = dot(aflag, (iota((amino, chip_pairs), 0) == residue).astype(BF16))[0:1, :]
    key_pair = jnp.where(ilane > 0.5, key_pair, 0.0).astype(jnp.int32)
    slot = iota((slots, 1), 0)
    gather = jnp.where(
        (key_pair == side * part + slot // block_rows + 1) & (lane_pair // amino == lax.rem(slot, block_rows)),
        1.0,
        0.0,
    ).astype(BF16)
    eye = iota((amino, amino), 0) == iota((amino, amino), 1)
    wide_key = jnp.broadcast_to(lane_keys(amino), (amino, amino))
    key_col = jnp.sum(jnp.where(eye, wide_key, 0.0), axis=1, keepdims=True).astype(jnp.int32)
    key_col = jnp.concatenate([key_col] * rows, axis=0)
    col = iota((1, nb * slots), 1)
    expand = jnp.where(
        (key_col == (nb - 1 - col // slots) * part + lax.rem(col, slots) // block_rows + 1)
        & (iota((pairs, 1), 0) // amino + branch * rows == lax.rem(col, block_rows)),
        1.0,
        0.0,
    ).astype(BF16)
    expand = jnp.concatenate([expand, expand], axis=1)
    arrived(class_all.at[other], pair_rsem.at[0])
    arrived(couple_all.at[other], pair_rsem.at[1])
    bins = embed_ref.shape[0]
    hot = []
    for b in range(nb):
        for i in range(rows):
            column = jnp.sum(
                jnp.where(eye, class_all[b, i : i + 1, :], 0).astype(F32), axis=1, keepdims=True
            ).astype(jnp.int32)
            hot.append(jnp.where(column == iota((amino, bins), 1), 1.0, 0.0))
    onehot = jnp.concatenate(hot, axis=0).astype(BF16)
    couple = couple_all[...].reshape(chip_pairs, width)
    base_buf[...] = (couple.astype(F32) + dot(onehot, embed_ref[...])).reshape(nb, pairs, width)
    base_c = dot(gather, couple) + dot(dot(gather, onehot).astype(BF16), embed_ref[...])

    if redo:

        @pl.when(dap == end)
        def _():
            base_send[...] = base_c.astype(BF16)

        push(base_send, base_last, base_sems.at[0], base_sems.at[1], (branch, 0), dap == end)

    for z in chips:
        d = branch * nz + z
        arrived(left_all.at[d], left_rsem.at[z - (z > dap)])
        push(left_all.at[d], left_all.at[d], pass_sems.at[0], pass_sems.at[1], partner)
    if redo:
        arrived(left_last.at[: nz - 1], last_sems.at[1], dap == 0)
        lasts = left_last.at[pl.ds(branch * nz, nz)]
        push(lasts, lasts, last_sems.at[2], last_sems.at[3], partner, dap == 0)
    if even:
        arrived(right_all.at[: n - 1], right_sems.at[1])
    else:
        arrived(right_all.at[: n - 1], right_sems.at[1], branch == wide)
        arrived(right_all.at[: n - 1, :least], right_sems.at[1], branch != wide)
    arrived(left_all.at[:nz], pass_sems.at[1])
    arrived(flag_all.at[: n - 1], flag_sems.at[1])

    number = jnp.maximum(jnp.sum(flag_all[...], axis=0), 1.0)
    right = jnp.concatenate([right_all[:, t].reshape(n * seqs, LANES) for t in range(groups)], axis=1)
    lane = iota((1, LANES), 1)

    def middle(left_ref, base):
        left = jnp.concatenate([left_ref[:, b].reshape(n * seqs, LANES) for b in range(nb)], axis=1)
        outer = lax.dot_general(left, right, (((0,), (0,)), ((), ())), preferred_element_type=F32)
        for t in range(groups):
            for i in range(block_rows):
                outer_buf[t, pl.ds(i * (inner + 1), inner), :] = outer[
                    i * inner : (i + 1) * inner, t * LANES : (t + 1) * LANES
                ]
        parts = [[] for _ in range(part)]
        for t in range(groups):
            for q in range(inner // reps):
                block = [outer_buf[t, pl.ds(q * reps + g, block_rows, stride=inner + 1), :] for g in range(reps)]
                span = reps // 2
                while span:
                    upper = (lane // (span * inner)) % 2 == 1
                    new = list(block)
                    for a in range(reps):
                        if a & span:
                            continue
                        b = a | span
                        shift = span * inner
                        if 2 * shift == LANES:
                            moved = pltpu.roll(jnp.where(upper, block[a], block[b]), shift, 1)
                            new[a] = jnp.where(upper, moved, block[a])
                            new[b] = jnp.where(upper, block[b], moved)
                        else:
                            new[a] = jnp.where(upper, pltpu.roll(block[b], shift, 1), block[a])
                            new[b] = jnp.where(upper, block[b], pltpu.roll(block[a], LANES - shift, 1))
                    block = new
                    span //= 2
                for g in range(reps):
                    parts[t * reps + g].append(block[g])
        packed = jnp.concatenate([jnp.concatenate(p, axis=1) for p in parts], axis=0).astype(BF16)
        product = dot(packed, tall_ref[:long]) / number
        pair_c = standardize(base + product, gain_ref[0]).astype(BF16)
        right_two = dot(pair_c, wedge_ref[:, 2 * width :])
        tri_right = jax.nn.sigmoid(right_two[:, :width]) * right_two[:, width:]
        return product, pair_c, tri_right.astype(BF16)

    product, pair_c, tri_all[dap] = middle(left_all, base_c)
    full = None if even else branch == wide
    short = None if even else branch != wide

    def tri_block(z, size):
        return tri_all.at[z, :size]

    for z in chips:
        skip = redo & (dap == end) & (z == 0)
        if even:
            push(tri_all.at[dap], tri_all.at[dap], tri_ssem.at[0], tri_rsem.at[rank_at(z)], (branch, z), ~skip)
        else:
            for size, when in ((slots, full), (firm, short)):
                push(
                    tri_block(dap, size), tri_block(dap, size), tri_ssem.at[0], tri_rsem.at[rank_at(z)], (branch, z),
                    when & ~skip,
                )

    product_all[branch] = product
    share(product_all, 2)
    left_two = dot(pair_c, wedge_ref[:, : 2 * width])
    edge_buf[...] = (jax.nn.sigmoid(left_two[:, :width]) * left_two[:, width:]).astype(BF16).astype(F32)
    for i in range(block_rows):
        for k in range(part):
            row = edge_buf[k * block_rows + i : k * block_rows + i + 1, :]
            spread_buf[i, k * SUB : (k + 1) * SUB, :] = jnp.broadcast_to(row, (SUB, width))

    def triangle(z, side, store):
        block = tri_all[z].astype(F32)
        for i in range(rows):
            both = spread_buf[side * rows + i] * block
            store[z, i] = jnp.sum(both.reshape(part, SUB, width), axis=0)

    def contribute(z):
        triangle(z, other, part_send)
        push(part_send.at[z], part_in.at[z], part_ssem.at[0], part_rsem.at[0], partner)
        triangle(z, branch, own_buf)

    def settle(z):
        for i in range(rows):
            total = own_buf[z, i] + part_in[z, i]
            for b in range(nb):
                row = i * amino + (b * nz + z) * rows
                tri_buf[pl.ds(pl.multiple_of(row, rows), rows), :] = total[b * rows : (b + 1) * rows]

    contribute(dap)
    if redo:

        @pl.when(dap == 0)
        def _():
            arrived(left_last.at[:nz], last_sems.at[3])
            arrived(base_last, base_sems.at[1])
            tri_all[end] = middle(left_last, base_last[...].astype(F32))[2]
            contribute(end)

    def refresh():
        arrived(product_all.at[other], pair_rsem.at[2])
        whole = product_all[...].reshape(nb * slots, width)
        high = whole.astype(BF16)
        rest = (whole - high.astype(F32)).astype(BF16)
        updated = base_buf[branch] + dot(expand, jnp.concatenate([high, rest], axis=0))
        pair = standardize(updated, gain_ref[0]).astype(BF16)
        updated_buf[...] = updated
        gate_buf[...] = jax.nn.sigmoid(dot(pair, tall_ref[long : long + width]))

    pl.when(dap != 0)(refresh)
    late = [jnp.where(dap == 0, k + 1, (k + 1 + (k + 1 >= dap)) % nz) for k in range(nz - 1)]
    late = [jnp.where((dap == 0) | (k < nz - 2), z, 0) for k, z in enumerate(late)]
    for k, z in enumerate(late):
        skip = redo & (dap == 0) & (z == end)

        @pl.when(~skip)
        def _():
            if even:
                arrived(tri_all.at[z], tri_rsem.at[z - (z > dap)])
            else:
                arrived(tri_block(z, slots), tri_rsem.at[z - (z > dap)], full)
                arrived(tri_block(z, firm), tri_rsem.at[z - (z > dap)], short)
            contribute(z)
    pl.when(dap == 0)(refresh)
    arrived(part_in, part_rsem.at[0])
    for z in range(nz):
        settle(z)
    tri = standardize(tri_buf[...], gain_ref[1]).astype(BF16)
    out_ref[...] = (updated_buf[...] + gate_buf[...] * dot(tri, tall_ref[long + width :])).astype(BF16)
    for b in range(nb):
        size = most if even or b == wide else least
        drain(right_all.at[: nz - 1, :size], right_sems.at[0])
        drain(right_all.at[:1, :size], right_sems.at[0], branch != b)
    drain(left_all.at[: n - 1], pass_sems.at[0])
    drain(flag_all.at[: n - 1], flag_sems.at[0])
    if redo:
        drain(left_last.at[0], last_sems.at[0], dap != 0)
        drain(left_last.at[:nz], last_sems.at[2], dap == 0)
        drain(base_send, base_sems.at[0], dap == end)
    for fewer, last in ((1, redo & (dap == end)), (0, ~(redo & (dap == end)))):
        if even:
            drain(tri_all.at[: nz - 1 - fewer], tri_ssem.at[0], last)
        else:
            drain(tri_all.at[: nz - 1 - fewer], tri_ssem.at[0], last & full)
            drain(tri_all.at[: nz - 1 - fewer, :firm], tri_ssem.at[0], last & short)
    drain(part_send, part_ssem.at[0])
    for k, ref in enumerate((class_all, couple_all, product_all)):
        drain(ref.at[branch], pair_ssem.at[k])


def on_device(nb, nz, x, hflags, aflags, classes, couple, hgain, wl, wr, wout, embed, cgain, wedge, wgate, wfin, tgain):
    n = nb * nz
    seqs, amino, depth = x.shape
    rows, _, width = couple.shape
    inner = wl.shape[1]
    live = amino - 3 * amino // 8
    groups = -(-(live // (LANES // inner)) // nb)
    part = groups * (LANES // inner)
    slots = part * nb * rows
    dma = pltpu.SemaphoreType.DMA
    operands = (
        x.reshape(seqs * amino, depth), hflags.reshape(1, seqs), aflags.reshape(1, amino), classes,
        couple.reshape(rows * amino, width), hgain.reshape(1, depth), wl.T, wr.T, wout, embed,
        cgain.reshape(1, width), wedge, wgate, wfin, tgain.reshape(1, width),
    )
    shapes = [a.shape for a in operands]
    shapes[3], shapes[4] = (nb, *shapes[3]), (nb, *shapes[4])
    held = [pltpu.VMEM(shapes[k], operands[k].dtype) for k in range(6)] + [
        pltpu.VMEM((2, inner, depth), BF16),
        pltpu.VMEM((inner * inner + 2 * width, width), BF16),
        pltpu.VMEM(shapes[9], BF16),
        pltpu.VMEM((2, 1, width), F32),
        pltpu.VMEM(shapes[11], BF16),
    ]
    out = pl.pallas_call(
        functools.partial(kernel, nb, nz),
        out_shape=pltpu.VMEM((rows * amino, width), BF16),
        in_specs=[pl.BlockSpec(memory_space=pl.ANY)] * OPERANDS,
        out_specs=pl.BlockSpec(memory_space=pltpu.VMEM),
        scratch_shapes=held
        + [
            dma((HELD,)),
            pltpu.VMEM((n, 1, LANES), F32),
            pltpu.VMEM((nb, groups, seqs, LANES), BF16),
            pltpu.VMEM((n, groups, seqs, LANES), BF16),
            pltpu.VMEM((nz, nb, seqs, LANES), BF16),
            pltpu.VMEM((n, nb, seqs, LANES), BF16),
            pltpu.VMEM((n, nb, seqs, LANES), BF16),
            pltpu.VMEM((nz, slots, width), BF16),
            pltpu.VMEM((seqs * (amino + 1), LANES), F32),
            pltpu.VMEM((groups, nb * rows * (inner + 1), LANES), F32),
            pltpu.VMEM((nb, rows * amino, width), F32),
            pltpu.VMEM((slots, width), BF16),
            pltpu.VMEM((slots, width), BF16),
            pltpu.VMEM((nb, slots, width), F32),
            pltpu.VMEM((slots, width), F32),
            pltpu.VMEM((nb * rows, slots, width), F32),
            pltpu.VMEM((nz, rows, SUB, width), F32),
            pltpu.VMEM((nz, rows, SUB, width), F32),
            pltpu.VMEM((nz, rows, SUB, width), F32),
            pltpu.VMEM((rows * amino, width), F32),
            pltpu.VMEM((rows * amino, width), F32),
            pltpu.VMEM((rows * amino, width), F32),
        ]
        + [dma((2,)), dma((2,)), dma((2,)), dma((4,)), dma((2,)), dma((nz - 1,))]
        + [dma((1,)), dma((nz - 1,)), dma((1,)), dma((1,)), dma((3,)), dma((3,))]
        + [pltpu.SemaphoreType.REGULAR((nz - 1,))],
        compiler_params=pltpu.CompilerParams(collective_id=0, has_side_effects=True),
    )(*operands)
    return out.reshape(rows, amino, width)


def solution(mesh):
    split = ("rep", "branch", "dap")
    placed = (
        P(split, None, None), P(split), P("rep"), P(split, None), P(split, None, None),
        P(), P(), P(), P(), P(), P(), P(), P(), P(), P(),
    )
    return jax.shard_map(
        functools.partial(on_device, mesh.shape["branch"], mesh.shape["dap"]),
        mesh=mesh,
        in_specs=placed,
        out_specs=P(split, None, None),
        check_vma=False,
    )
```

```python
import functools

import jax
import jax.numpy as jnp
from jax import lax
from jax.experimental import pallas as pl
from jax.experimental.pallas import tpu as pltpu
from jax.sharding import PartitionSpec as P

F32 = jnp.float32
BF16 = jnp.bfloat16
MESH = pl.DeviceIdType.MESH
OPERANDS = 15
HELD = 11
LANES = 128
SUB = 8


def iota(shape, axis):
    return lax.broadcasted_iota(jnp.int32, shape, axis)


def dot(a, b):
    return jnp.dot(a, b, preferred_element_type=F32)


def standardize(values, gain):
    mean = jnp.mean(values, axis=-1, keepdims=True)
    centred = values - mean
    spread = jnp.mean(centred * centred, axis=-1, keepdims=True)
    return centred * lax.rsqrt(spread + 1e-05) * gain


def kernel(
    nb, nz,
    *refs,
):
    operands, out_ref, held = refs[:OPERANDS], refs[OPERANDS], refs[OPERANDS + 1 : OPERANDS + 1 + HELD]
    in_sem, *scratch = refs[OPERANDS + 1 + HELD :]
    x_ref, hflag_ref, aflag_ref, class_all, couple_all, hgain_ref, side_ref, tall_ref, embed_ref, gain_ref, wedge_ref = held
    (
    flag_all, right_send, right_all, left_send, left_all, left_last, tri_all, y_left, outer_buf,
    base_buf, base_send, base_last, product_all, edge_buf, spread_buf, own_buf, part_send, part_in, tri_buf, updated_buf, gate_buf,
    flag_sems, right_sems, pass_sems, last_sems, base_sems, left_rsem, tri_ssem, tri_rsem, part_ssem, part_rsem,
    pair_ssem, pair_rsem, ready,
    ) = scratch
    n = nb * nz
    branch = lax.axis_index("branch")
    dap = lax.axis_index("dap")
    me = branch * nz + dap
    amino = aflag_ref.shape[1]
    seqs = hflag_ref.shape[1]
    rows = class_all.shape[1]
    inner = side_ref.shape[1]
    width = couple_all.shape[2]
    reps = LANES // inner
    live = amino - 3 * amino // 8
    tiles = live // reps
    groups = -(-tiles // nb)
    even = tiles % nb == 0
    part = groups * reps
    most = groups
    least = most if even else most - 1
    block_rows = nb * rows
    slots = part * block_rows
    firm = slots - reps * block_rows
    pairs = rows * amino
    side = nb - 1 - branch
    wide = nb - 1
    chips = [k + (k >= dap) for k in range(nz - 1)]
    redo = nz > 2
    end = nz - 1
    order = []
    for k in range(nz - 1):
        rank = jnp.where(dap == 0, nz - 2, jnp.where(dap == end, end, dap - 1))
        rank = k + (k >= rank)
        order.append(jnp.where(rank < nz - 2, rank + 1, jnp.where(rank == nz - 2, 0, end)))
    other = nb - 1 - branch
    partner = (other, dap)
    everyone = [partner] + [(b, z) for z in chips for b in (branch, other)]

    def rank_at(z):
        return dap - (dap > z)

    def index_of(peer):
        return peer[0] * nz + peer[1]

    def target(peer):
        return {"branch": peer[0], "dap": peer[1]}

    long = inner * inner
    homes = [
        (x_ref, 0), (hflag_ref, 1), (aflag_ref, 2), (class_all.at[branch], 3), (couple_all.at[branch], 4),
        (hgain_ref, 5), (side_ref.at[0], 6), (side_ref.at[1], 6), (tall_ref.at[:long], 7), (embed_ref, 8),
        (gain_ref.at[0], 9), (wedge_ref, 10), (tall_ref.at[long : long + width], 7),
        (tall_ref.at[long + width :], 7), (gain_ref.at[1], 9),
    ]
    whole_homes = {6: side_ref, 7: tall_ref, 9: gain_ref}
    for k in (2, 1, 0, 5, 6, 7, 8, 3, 4, 9, 10, 11, 12, 13, 14):
        home, sem = homes[k]
        pieces = 8 if k == 0 else 1
        for p in range(pieces):
            step = home.shape[0] // pieces
            source, target_ref = operands[k], home
            if pieces > 1:
                source, target_ref = source.at[pl.ds(p * step, step)], target_ref.at[pl.ds(p * step, step)]
            pltpu.make_async_copy(source, target_ref, in_sem.at[sem]).start()

    def loaded(*keys):
        for sem in sorted({homes[k][1] for k in keys}):
            ref = whole_homes[sem] if sem in whole_homes else next(home for home, at in homes if at == sem)
            pltpu.make_async_copy(ref, ref, in_sem.at[sem]).wait()

    barrier = pltpu.get_barrier_semaphore()
    pl.semaphore_signal(barrier, inc=1, device_id=target(partner), device_id_type=MESH)
    for b, z in everyone[1:]:

        @pl.when(z > dap)
        def _():
            pl.semaphore_signal(barrier, inc=1, device_id=target((b, z)), device_id_type=MESH)

    pl.semaphore_wait(barrier, dap * nb + 1)
    for b, z in everyone[1:]:

        @pl.when(z < dap)
        def _():
            pl.semaphore_signal(ready.at[dap - 1], inc=1, device_id=target((b, z)), device_id_type=MESH)

    if not even:

        @pl.when(branch != wide)
        def _():
            right_all[:, least:] = jnp.zeros((n, most - least, seqs, LANES), BF16)
            tri_all[:, firm:, :] = jnp.zeros((nz, slots - firm, width), BF16)

    loaded(2, 1)
    aflag = jnp.broadcast_to(aflag_ref[...].astype(F32), (SUB, amino)).astype(BF16)
    hflag32 = hflag_ref[...].astype(F32)
    hflag = jnp.broadcast_to(hflag32, (SUB, seqs)).astype(BF16)

    def lane_keys(lanes):
        r = iota((amino, lanes), 0)
        k = lax.rem(iota((amino, lanes), 1), amino)
        count = dot(aflag, (r <= k).astype(BF16))
        alive = dot(aflag, (r == k).astype(BF16))
        return (count * alive)[0:1, :]

    flag_all[me] = jnp.broadcast_to(jnp.sum(hflag32, axis=1, keepdims=True), (1, LANES))

    total = seqs * amino
    span = SUB * amino
    key_x = lane_keys(span)
    hlane = dot(hflag, (iota((seqs, total), 0) == iota((seqs, total), 1) // amino).astype(BF16))[0:1, :]
    gather_right = []
    for h in range(seqs // SUB):
        code = (key_x - 1.0) * SUB + (iota((1, span), 1) // amino).astype(F32)
        code = jnp.where(hlane[:, h * span : (h + 1) * span] * key_x > 0.5, code, -1.0).astype(jnp.int32)
        gather_right.append(jnp.where(iota((live * SUB, 1), 0) == code, 1.0, 0.0).astype(BF16))
    lane_group = iota((1, LANES), 1) // inner
    alane = dot(
        aflag,
        (iota((amino, amino * inner), 0) == iota((amino, amino * inner), 1) // inner).astype(BF16),
    )[0:1, :]

    loaded(0, 5, 6, 7)
    depth = x_ref.shape[1]
    mean = dot(x_ref[...], jnp.ones((depth, LANES), BF16)) * (1.0 / depth)
    centred = x_ref[...].astype(F32) - jnp.concatenate([mean] * (depth // LANES), axis=1)
    spread = jnp.mean(centred * centred, axis=-1, keepdims=True)
    normed = (centred * lax.rsqrt(spread + 1e-05) * hgain_ref[...]).astype(BF16)
    w_both = jnp.concatenate([side_ref[0]] * reps + [side_ref[1]] * reps, axis=0)
    sides = lax.dot_general(
        normed, w_both, (((1,), (1,)), ((), ())), preferred_element_type=F32
    )
    for i in range(seqs):
        y_left[pl.ds(i * (amino + 1), amino), :] = sides[i * amino : (i + 1) * amino, :LANES]
    for d in range(n):
        block = y_left[pl.ds(d * rows, seqs, stride=amino + 1), :]
        for g in range(1, rows):
            block = jnp.where(
                lane_group == g, y_left[pl.ds(d * rows + g, seqs, stride=amino + 1), :], block
            )
        left_send[d % nz, d // nz] = (block * alane[:, d * LANES : (d + 1) * LANES]).astype(BF16)

    def guarded(when, act):
        if when is None:
            act()
        else:
            pl.when(when)(act)

    def push(src, dst, ssem, rsem, peer, when=None):
        copy = pltpu.make_async_remote_copy(
            src_ref=src, dst_ref=dst, send_sem=ssem, recv_sem=rsem,
            device_id=target(peer), device_id_type=MESH,
        )
        guarded(when, copy.start)

    def push_left(z):
        push(left_send.at[z], left_all.at[me], pass_sems.at[0], left_rsem.at[rank_at(z)], (branch, z))

    first_left = order[:1]
    for z in first_left:
        pl.when(z < dap)(functools.partial(push_left, z))
    right_rows = [
        dot(gather, sides[h * span : (h + 1) * span, LANES:].astype(BF16)) for h, gather in enumerate(gather_right)
    ]

    def right_of(k):
        return jnp.concatenate([part_rows[k * SUB : (k + 1) * SUB] for part_rows in right_rows], axis=0)

    for b in range(nb):
        for t in range(min(groups, tiles - (nb - 1 - b) * groups)):
            begin = (nb - 1 - b) * part + t * reps
            block = right_of(begin)
            for g in range(1, reps):
                block = jnp.where(lane_group == g, right_of(begin + g), block)
            right_send[b, t] = block.astype(BF16)

    def drain(ref, ssem, when=None):
        wait = pltpu.make_async_remote_copy(
            src_ref=ref, dst_ref=ref, send_sem=ssem, recv_sem=ssem,
            device_id=target(partner), device_id_type=MESH,
        ).wait_send
        guarded(when, wait)

    def arrived(ref, rsem, when=None):
        wait = pltpu.make_async_remote_copy(
            src_ref=ref, dst_ref=ref, send_sem=rsem,
            recv_sem=rsem, device_id=target(partner), device_id_type=MESH,
        ).wait_recv
        guarded(when, wait)

    def share(ref, k):
        push(ref.at[branch], ref.at[branch], pair_ssem.at[k], pair_rsem.at[k], partner)

    def push_right(b, z, when=None):
        size = most if even or b == wide else least
        push(
            right_send.at[b, :size], right_all.at[me, :size], right_sems.at[0], right_sems.at[1], (b, z), when
        )

    for k, z in enumerate(order):

        @pl.when(z > dap)
        def _():
            pl.semaphore_wait(ready.at[z - 1], nb)

        pl.when(z > dap)(functools.partial(push_left, z))
        if redo:
            push(left_send.at[end], left_last.at[me], last_sems.at[0], last_sems.at[1], (branch, 0), z == 0)
        for b in range(nb):
            push(flag_all.at[me], flag_all.at[me], flag_sems.at[0], flag_sems.at[1], (b, z))
        for b in range(nb):
            push_right(b, z)
            if b == 0 and k + 1 < len(order):
                pl.when(order[k + 1] < dap)(functools.partial(push_left, order[k + 1]))
    for b in range(nb):
        push_right(b, dap, branch != b)
    push(left_send.at[dap], left_all.at[me], pass_sems.at[0], pass_sems.at[1], partner)
    push(flag_all.at[me], flag_all.at[me], flag_sems.at[0], flag_sems.at[1], partner)
    loaded(3, 4)
    share(class_all, 0)
    share(couple_all, 1)
    left_all[me] = left_send[dap]
    right_all[me, :least] = right_send[branch, :least]
    if not even:

        @pl.when(branch == wide)
        def _():
            right_all[me, least:] = right_send[wide, least:]

    if redo:

        @pl.when(dap == 0)
        def _():
            left_last[me] = left_send[end]

    loaded(8, 9, 10, 11)
    chip_pairs = nb * pairs
    lane_pair = iota((1, chip_pairs), 1)
    key_pair = lane_keys(chip_pairs)
    residue = (lane_pair // pairs * nz + dap) * rows + lax.rem(lane_pair // amino, rows)
    ilane = dot(aflag, (iota((amino, chip_pairs), 0) == residue).astype(BF16))[0:1, :]
    key_pair = jnp.where(ilane > 0.5, key_pair, 0.0).astype(jnp.int32)
    slot = iota((slots, 1), 0)
    gather = jnp.where(
        (key_pair == side * part + slot // block_rows + 1) & (lane_pair // amino == lax.rem(slot, block_rows)),
        1.0,
        0.0,
    ).astype(BF16)
    eye = iota((amino, amino), 0) == iota((amino, amino), 1)
    wide_key = jnp.broadcast_to(lane_keys(amino), (amino, amino))
    key_col = jnp.sum(jnp.where(eye, wide_key, 0.0), axis=1, keepdims=True).astype(jnp.int32)
    key_col = jnp.concatenate([key_col] * rows, axis=0)
    col = iota((1, nb * slots), 1)
    expand = jnp.where(
        (key_col == (nb - 1 - col // slots) * part + lax.rem(col, slots) // block_rows + 1)
        & (iota((pairs, 1), 0) // amino + branch * rows == lax.rem(col, block_rows)),
        1.0,
        0.0,
    ).astype(BF16)
    expand = jnp.concatenate([expand, expand], axis=1)
    arrived(class_all.at[other], pair_rsem.at[0])
    arrived(couple_all.at[other], pair_rsem.at[1])
    bins = embed_ref.shape[0]
    hot = []
    for b in range(nb):
        for i in range(rows):
            column = jnp.sum(
                jnp.where(eye, class_all[b, i : i + 1, :], 0).astype(F32), axis=1, keepdims=True
            ).astype(jnp.int32)
            hot.append(jnp.where(column == iota((amino, bins), 1), 1.0, 0.0))
    onehot = jnp.concatenate(hot, axis=0).astype(BF16)
    couple = couple_all[...].reshape(chip_pairs, width)
    base_buf[...] = (couple.astype(F32) + dot(onehot, embed_ref[...])).reshape(nb, pairs, width)
    base_c = dot(gather, couple) + dot(dot(gather, onehot).astype(BF16), embed_ref[...])

    if redo:

        @pl.when(dap == end)
        def _():
            base_send[...] = base_c.astype(BF16)

        push(base_send, base_last, base_sems.at[0], base_sems.at[1], (branch, 0), dap == end)

    for z in chips:
        d = branch * nz + z
        arrived(left_all.at[d], left_rsem.at[z - (z > dap)])
        push(left_all.at[d], left_all.at[d], pass_sems.at[0], pass_sems.at[1], partner)
    if redo:
        arrived(left_last.at[: nz - 1], last_sems.at[1], dap == 0)
        lasts = left_last.at[pl.ds(branch * nz, nz)]
        push(lasts, lasts, last_sems.at[2], last_sems.at[3], partner, dap == 0)
    if even:
        arrived(right_all.at[: n - 1], right_sems.at[1])
    else:
        arrived(right_all.at[: n - 1], right_sems.at[1], branch == wide)
        arrived(right_all.at[: n - 1, :least], right_sems.at[1], branch != wide)
    arrived(left_all.at[:nz], pass_sems.at[1])
    arrived(flag_all.at[: n - 1], flag_sems.at[1])

    number = jnp.maximum(jnp.sum(flag_all[...], axis=0), 1.0)
    right = jnp.concatenate([right_all[:, t].reshape(n * seqs, LANES) for t in range(groups)], axis=1)
    lane = iota((1, LANES), 1)

    def middle(left_ref, base):
        left = jnp.concatenate([left_ref[:, b].reshape(n * seqs, LANES) for b in range(nb)], axis=1)
        outer = lax.dot_general(left, right, (((0,), (0,)), ((), ())), preferred_element_type=F32)
        for t in range(groups):
            for i in range(block_rows):
                outer_buf[t, pl.ds(i * (inner + 1), inner), :] = outer[
                    i * inner : (i + 1) * inner, t * LANES : (t + 1) * LANES
                ]
        parts = [[] for _ in range(part)]
        for t in range(groups):
            for q in range(inner // reps):
                block = [outer_buf[t, pl.ds(q * reps + g, block_rows, stride=inner + 1), :] for g in range(reps)]
                span = reps // 2
                while span:
                    upper = (lane // (span * inner)) % 2 == 1
                    new = list(block)
                    for a in range(reps):
                        if a & span:
                            continue
                        b = a | span
                        shift = span * inner
                        if 2 * shift == LANES:
                            moved = pltpu.roll(jnp.where(upper, block[a], block[b]), shift, 1)
                            new[a] = jnp.where(upper, moved, block[a])
                            new[b] = jnp.where(upper, block[b], moved)
                        else:
                            new[a] = jnp.where(upper, pltpu.roll(block[b], shift, 1), block[a])
                            new[b] = jnp.where(upper, block[b], pltpu.roll(block[a], LANES - shift, 1))
                    block = new
                    span //= 2
                for g in range(reps):
                    parts[t * reps + g].append(block[g])
        packed = jnp.concatenate([jnp.concatenate(p, axis=1) for p in parts], axis=0).astype(BF16)
        product = dot(packed, tall_ref[:long]) / number
        pair_c = standardize(base + product, gain_ref[0]).astype(BF16)
        right_two = dot(pair_c, wedge_ref[:, 2 * width :])
        tri_right = jax.nn.sigmoid(right_two[:, :width]) * right_two[:, width:]
        return product, pair_c, tri_right.astype(BF16)

    product, pair_c, tri_all[dap] = middle(left_all, base_c)
    full = None if even else branch == wide
    short = None if even else branch != wide

    def tri_block(z, size):
        return tri_all.at[z, :size]

    for z in chips:
        skip = redo & (dap == end) & (z == 0)
        if even:
            push(tri_all.at[dap], tri_all.at[dap], tri_ssem.at[0], tri_rsem.at[rank_at(z)], (branch, z), ~skip)
        else:
            for size, when in ((slots, full), (firm, short)):
                push(
                    tri_block(dap, size), tri_block(dap, size), tri_ssem.at[0], tri_rsem.at[rank_at(z)], (branch, z),
                    when & ~skip,
                )

    product_all[branch] = product
    share(product_all, 2)
    left_two = dot(pair_c, wedge_ref[:, : 2 * width])
    edge_buf[...] = (jax.nn.sigmoid(left_two[:, :width]) * left_two[:, width:]).astype(BF16).astype(F32)
    for i in range(block_rows):
        for k in range(part):
            row = edge_buf[k * block_rows + i : k * block_rows + i + 1, :]
            spread_buf[i, k * SUB : (k + 1) * SUB, :] = jnp.broadcast_to(row, (SUB, width))

    def triangle(z, side, store):
        block = tri_all[z].astype(F32)
        for i in range(rows):
            both = spread_buf[side * rows + i] * block
            store[z, i] = jnp.sum(both.reshape(part, SUB, width), axis=0)

    def contribute(z):
        triangle(z, other, part_send)
        push(part_send.at[z], part_in.at[z], part_ssem.at[0], part_rsem.at[0], partner)
        triangle(z, branch, own_buf)

    def settle(z):
        for i in range(rows):
            total = own_buf[z, i] + part_in[z, i]
            for b in range(nb):
                row = i * amino + (b * nz + z) * rows
                tri_buf[pl.ds(pl.multiple_of(row, rows), rows), :] = total[b * rows : (b + 1) * rows]

    contribute(dap)
    if redo:

        @pl.when(dap == 0)
        def _():
            arrived(left_last.at[:nz], last_sems.at[3])
            arrived(base_last, base_sems.at[1])
            tri_all[end] = middle(left_last, base_last[...].astype(F32))[2]
            contribute(end)

    def refresh():
        arrived(product_all.at[other], pair_rsem.at[2])
        whole = product_all[...].reshape(nb * slots, width)
        high = whole.astype(BF16)
        rest = (whole - high.astype(F32)).astype(BF16)
        updated = base_buf[branch] + dot(expand, jnp.concatenate([high, rest], axis=0))
        pair = standardize(updated, gain_ref[0]).astype(BF16)
        updated_buf[...] = updated
        gate_buf[...] = jax.nn.sigmoid(dot(pair, tall_ref[long : long + width]))

    pl.when(dap != 0)(refresh)
    late = [jnp.where(dap == 0, end - k, (k + 1 + (k + 1 >= dap)) % nz) for k in range(nz - 1)]
    late = [jnp.where((dap == 0) | (k < nz - 2), z, 0) for k, z in enumerate(late)]
    for k, z in enumerate(late):
        skip = redo & (dap == 0) & (z == end)

        @pl.when(~skip)
        def _():
            if even:
                arrived(tri_all.at[z], tri_rsem.at[z - (z > dap)])
            else:
                arrived(tri_block(z, slots), tri_rsem.at[z - (z > dap)], full)
                arrived(tri_block(z, firm), tri_rsem.at[z - (z > dap)], short)
            contribute(z)
    pl.when(dap == 0)(refresh)
    arrived(part_in, part_rsem.at[0])
    for z in range(nz):
        settle(z)
    tri = standardize(tri_buf[:pairs], gain_ref[1]).astype(BF16)
    out_ref[...] = (updated_buf[...] + gate_buf[...] * dot(tri, tall_ref[long + width :])).astype(BF16)
    for b in range(nb):
        size = most if even or b == wide else least
        drain(right_all.at[: nz - 1, :size], right_sems.at[0])
        drain(right_all.at[:1, :size], right_sems.at[0], branch != b)
    drain(left_all.at[: n - 1], pass_sems.at[0])
    drain(flag_all.at[: n - 1], flag_sems.at[0])
    if redo:
        drain(left_last.at[0], last_sems.at[0], dap != 0)
        drain(left_last.at[:nz], last_sems.at[2], dap == 0)
        drain(base_send, base_sems.at[0], dap == end)
    for fewer, last in ((1, redo & (dap == end)), (0, ~(redo & (dap == end)))):
        if even:
            drain(tri_all.at[: nz - 1 - fewer], tri_ssem.at[0], last)
        else:
            drain(tri_all.at[: nz - 1 - fewer], tri_ssem.at[0], last & full)
            drain(tri_all.at[: nz - 1 - fewer, :firm], tri_ssem.at[0], last & short)
    drain(part_send, part_ssem.at[0])
    for k, ref in enumerate((class_all, couple_all, product_all)):
        drain(ref.at[branch], pair_ssem.at[k])


def on_device(nb, nz, x, hflags, aflags, classes, couple, hgain, wl, wr, wout, embed, cgain, wedge, wgate, wfin, tgain):
    n = nb * nz
    seqs, amino, depth = x.shape
    rows, _, width = couple.shape
    inner = wl.shape[1]
    live = amino - 3 * amino // 8
    groups = -(-(live // (LANES // inner)) // nb)
    part = groups * (LANES // inner)
    slots = part * nb * rows
    dma = pltpu.SemaphoreType.DMA
    operands = (
        x.reshape(seqs * amino, depth), hflags.reshape(1, seqs), aflags.reshape(1, amino), classes,
        couple.reshape(rows * amino, width), hgain.reshape(1, depth), wl.T, wr.T, wout, embed,
        cgain.reshape(1, width), wedge, wgate, wfin, tgain.reshape(1, width),
    )
    shapes = [a.shape for a in operands]
    shapes[3], shapes[4] = (nb, *shapes[3]), (nb, *shapes[4])
    held = [pltpu.VMEM(shapes[k], operands[k].dtype) for k in range(6)] + [
        pltpu.VMEM((2, inner, depth), BF16),
        pltpu.VMEM((inner * inner + 2 * width, width), BF16),
        pltpu.VMEM(shapes[9], BF16),
        pltpu.VMEM((2, 1, width), F32),
        pltpu.VMEM(shapes[11], BF16),
    ]
    out = pl.pallas_call(
        functools.partial(kernel, nb, nz),
        out_shape=pltpu.VMEM((rows * amino, width), BF16),
        in_specs=[pl.BlockSpec(memory_space=pl.ANY)] * OPERANDS,
        out_specs=pl.BlockSpec(memory_space=pltpu.VMEM),
        scratch_shapes=held
        + [
            dma((HELD,)),
            pltpu.VMEM((n, 1, LANES), F32),
            pltpu.VMEM((nb, groups, seqs, LANES), BF16),
            pltpu.VMEM((n, groups, seqs, LANES), BF16),
            pltpu.VMEM((nz, nb, seqs, LANES), BF16),
            pltpu.VMEM((n, nb, seqs, LANES), BF16),
            pltpu.VMEM((n, nb, seqs, LANES), BF16),
            pltpu.VMEM((nz, slots, width), BF16),
            pltpu.VMEM(((seqs + 1) * (amino + 1), LANES), F32),
            pltpu.VMEM((groups, (nb * rows + 1) * (inner + 1), LANES), F32),
            pltpu.VMEM((nb, rows * amino, width), F32),
            pltpu.VMEM((slots, width), BF16),
            pltpu.VMEM((slots, width), BF16),
            pltpu.VMEM((nb, slots, width), F32),
            pltpu.VMEM((slots, width), F32),
            pltpu.VMEM((nb * rows, slots, width), F32),
            pltpu.VMEM((nz, rows, SUB, width), F32),
            pltpu.VMEM((nz, rows, SUB, width), F32),
            pltpu.VMEM((nz, rows, SUB, width), F32),
            pltpu.VMEM((rows * amino + SUB, width), F32),
            pltpu.VMEM((rows * amino, width), F32),
            pltpu.VMEM((rows * amino, width), F32),
        ]
        + [dma((2,)), dma((2,)), dma((2,)), dma((4,)), dma((2,)), dma((nz - 1,))]
        + [dma((1,)), dma((nz - 1,)), dma((1,)), dma((1,)), dma((3,)), dma((3,))]
        + [pltpu.SemaphoreType.REGULAR((nz - 1,))],
        compiler_params=pltpu.CompilerParams(collective_id=0, has_side_effects=True),
    )(*operands)
    return out.reshape(rows, amino, width)


def solution(mesh):
    split = ("rep", "branch", "dap")
    placed = (
        P(split, None, None), P(split), P("rep"), P(split, None), P(split, None, None),
        P(), P(), P(), P(), P(), P(), P(), P(), P(), P(),
    )
    return jax.shard_map(
        functools.partial(on_device, mesh.shape["branch"], mesh.shape["dap"]),
        mesh=mesh,
        in_specs=placed,
        out_specs=P(split, None, None),
        check_vma=False,
    )
```

```python
import functools

import jax
import jax.numpy as jnp
from jax import lax
from jax.experimental import pallas as pl
from jax.experimental.pallas import tpu as pltpu
from jax.sharding import PartitionSpec as P

F32 = jnp.float32
BF16 = jnp.bfloat16
MESH = pl.DeviceIdType.MESH
OPERANDS = 15
HELD = 11
LANES = 128
SUB = 8


def iota(shape, axis):
    return lax.broadcasted_iota(jnp.int32, shape, axis)


def dot(a, b):
    return jnp.dot(a, b, preferred_element_type=F32)


def standardize(values, gain):
    mean = jnp.mean(values, axis=-1, keepdims=True)
    centred = values - mean
    spread = jnp.mean(centred * centred, axis=-1, keepdims=True)
    return centred * lax.rsqrt(spread + 1e-05) * gain


def kernel(
    nb, nz,
    *refs,
):
    operands, out_ref, held = refs[:OPERANDS], refs[OPERANDS], refs[OPERANDS + 1 : OPERANDS + 1 + HELD]
    in_sem, *scratch = refs[OPERANDS + 1 + HELD :]
    x_ref, hflag_ref, aflag_ref, class_all, couple_all, hgain_ref, side_ref, tall_ref, embed_ref, gain_ref, wedge_ref = held
    (
    flag_all, right_send, right_all, left_send, left_all, left_last, tri_all, y_left, outer_buf,
    base_buf, base_send, base_last, product_all, edge_buf, spread_buf, own_buf, part_send, part_in, tri_buf, updated_buf, gate_buf,
    flag_sems, right_sems, pass_sems, last_sems, base_sems, left_rsem, tri_ssem, tri_rsem, part_ssem, part_rsem,
    pair_ssem, pair_rsem, ready,
    ) = scratch
    n = nb * nz
    branch = lax.axis_index("branch")
    dap = lax.axis_index("dap")
    me = branch * nz + dap
    amino = aflag_ref.shape[1]
    seqs = hflag_ref.shape[1]
    rows = class_all.shape[1]
    inner = side_ref.shape[1]
    width = couple_all.shape[2]
    reps = LANES // inner
    live = amino - 3 * amino // 8
    tiles = live // reps
    groups = -(-tiles // nb)
    even = tiles % nb == 0
    part = groups * reps
    most = groups
    least = most if even else most - 1
    block_rows = nb * rows
    slots = part * block_rows
    firm = slots - reps * block_rows
    pairs = rows * amino
    side = nb - 1 - branch
    wide = nb - 1
    chips = [k + (k >= dap) for k in range(nz - 1)]
    redo = nz > 2
    end = nz - 1
    order = []
    for k in range(nz - 1):
        rank = jnp.where(dap == 0, nz - 2, jnp.where(dap == end, end, dap - 1))
        rank = k + (k >= rank)
        order.append(jnp.where(rank < nz - 2, rank + 1, jnp.where(rank == nz - 2, 0, end)))
    other = nb - 1 - branch
    partner = (other, dap)
    everyone = [partner] + [(b, z) for z in chips for b in (branch, other)]

    def rank_at(z):
        return dap - (dap > z)

    def index_of(peer):
        return peer[0] * nz + peer[1]

    def target(peer):
        return {"branch": peer[0], "dap": peer[1]}

    long = inner * inner
    homes = [
        (x_ref, 0), (hflag_ref, 1), (aflag_ref, 2), (class_all.at[branch], 3), (couple_all.at[branch], 4),
        (hgain_ref, 5), (side_ref.at[0], 6), (side_ref.at[1], 6), (tall_ref.at[:long], 7), (embed_ref, 8),
        (gain_ref.at[0], 9), (wedge_ref, 10), (tall_ref.at[long : long + width], 7),
        (tall_ref.at[long + width :], 7), (gain_ref.at[1], 9),
    ]
    whole_homes = {6: side_ref, 7: tall_ref, 9: gain_ref}
    for k in (2, 1, 0, 5, 6, 7, 8, 3, 4, 9, 10, 11, 12, 13, 14):
        home, sem = homes[k]
        pieces = 8 if k == 0 else 1
        for p in range(pieces):
            step = home.shape[0] // pieces
            source, target_ref = operands[k], home
            if pieces > 1:
                source, target_ref = source.at[pl.ds(p * step, step)], target_ref.at[pl.ds(p * step, step)]
            pltpu.make_async_copy(source, target_ref, in_sem.at[sem]).start()

    def loaded(*keys):
        for sem in sorted({homes[k][1] for k in keys}):
            ref = whole_homes[sem] if sem in whole_homes else next(home for home, at in homes if at == sem)
            pltpu.make_async_copy(ref, ref, in_sem.at[sem]).wait()

    barrier = pltpu.get_barrier_semaphore()
    pl.semaphore_signal(barrier, inc=1, device_id=target(partner), device_id_type=MESH)
    for b, z in everyone[1:]:

        @pl.when(z > dap)
        def _():
            pl.semaphore_signal(barrier, inc=1, device_id=target((b, z)), device_id_type=MESH)

    pl.semaphore_wait(barrier, dap * nb + 1)
    for b, z in everyone[1:]:

        @pl.when(z < dap)
        def _():
            pl.semaphore_signal(ready.at[dap - 1], inc=1, device_id=target((b, z)), device_id_type=MESH)

    if not even:

        @pl.when(branch != wide)
        def _():
            right_all[:, least:] = jnp.zeros((n, most - least, seqs, LANES), BF16)
            tri_all[:, firm:, :] = jnp.zeros((nz, slots - firm, width), BF16)

    loaded(2, 1)
    aflag = jnp.broadcast_to(aflag_ref[...].astype(F32), (SUB, amino)).astype(BF16)
    hflag32 = hflag_ref[...].astype(F32)
    hflag = jnp.broadcast_to(hflag32, (SUB, seqs)).astype(BF16)

    def lane_keys(lanes):
        r = iota((amino, lanes), 0)
        k = lax.rem(iota((amino, lanes), 1), amino)
        count = dot(aflag, (r <= k).astype(BF16))
        alive = dot(aflag, (r == k).astype(BF16))
        return (count * alive)[0:1, :]

    flag_all[me] = jnp.broadcast_to(jnp.sum(hflag32, axis=1, keepdims=True), (1, LANES))

    total = seqs * amino
    span = SUB * amino
    key_x = lane_keys(span)
    hlane = dot(hflag, (iota((seqs, total), 0) == iota((seqs, total), 1) // amino).astype(BF16))[0:1, :]
    gather_right = []
    for h in range(seqs // SUB):
        code = (key_x - 1.0) * SUB + (iota((1, span), 1) // amino).astype(F32)
        code = jnp.where(hlane[:, h * span : (h + 1) * span] * key_x > 0.5, code, -1.0).astype(jnp.int32)
        gather_right.append(jnp.where(iota((live * SUB, 1), 0) == code, 1.0, 0.0).astype(BF16))
    lane_group = iota((1, LANES), 1) // inner
    alane = dot(
        aflag,
        (iota((amino, amino * inner), 0) == iota((amino, amino * inner), 1) // inner).astype(BF16),
    )[0:1, :]

    loaded(0, 5, 6, 7)
    depth = x_ref.shape[1]
    mean = dot(x_ref[...], jnp.ones((depth, LANES), BF16)) * (1.0 / depth)
    centred = x_ref[...].astype(F32) - jnp.concatenate([mean] * (depth // LANES), axis=1)
    spread = jnp.mean(centred * centred, axis=-1, keepdims=True)
    normed = (centred * lax.rsqrt(spread + 1e-05) * hgain_ref[...]).astype(BF16)
    w_both = jnp.concatenate([side_ref[0]] * reps + [side_ref[1]] * reps, axis=0)
    sides = lax.dot_general(
        normed, w_both, (((1,), (1,)), ((), ())), preferred_element_type=F32
    )
    for i in range(seqs):
        y_left[pl.ds(i * (amino + 1), amino), :] = sides[i * amino : (i + 1) * amino, :LANES]
    for d in range(n):
        block = y_left[pl.ds(d * rows, seqs, stride=amino + 1), :]
        for g in range(1, rows):
            block = jnp.where(
                lane_group == g, y_left[pl.ds(d * rows + g, seqs, stride=amino + 1), :], block
            )
        left_send[d % nz, d // nz] = (block * alane[:, d * LANES : (d + 1) * LANES]).astype(BF16)

    def guarded(when, act):
        if when is None:
            act()
        else:
            pl.when(when)(act)

    def push(src, dst, ssem, rsem, peer, when=None):
        copy = pltpu.make_async_remote_copy(
            src_ref=src, dst_ref=dst, send_sem=ssem, recv_sem=rsem,
            device_id=target(peer), device_id_type=MESH,
        )
        guarded(when, copy.start)

    def push_left(z):
        push(left_send.at[z], left_all.at[me], pass_sems.at[0], left_rsem.at[rank_at(z)], (branch, z))

    first_left = order[:1]
    for z in first_left:
        pl.when(z < dap)(functools.partial(push_left, z))
    right_rows = [
        dot(gather, sides[h * span : (h + 1) * span, LANES:].astype(BF16)) for h, gather in enumerate(gather_right)
    ]

    def right_of(k):
        return jnp.concatenate([part_rows[k * SUB : (k + 1) * SUB] for part_rows in right_rows], axis=0)

    for b in range(nb):
        for t in range(min(groups, tiles - (nb - 1 - b) * groups)):
            begin = (nb - 1 - b) * part + t * reps
            block = right_of(begin)
            for g in range(1, reps):
                block = jnp.where(lane_group == g, right_of(begin + g), block)
            right_send[b, t] = block.astype(BF16)

    def drain(ref, ssem, when=None):
        wait = pltpu.make_async_remote_copy(
            src_ref=ref, dst_ref=ref, send_sem=ssem, recv_sem=ssem,
            device_id=target(partner), device_id_type=MESH,
        ).wait_send
        guarded(when, wait)

    def arrived(ref, rsem, when=None):
        wait = pltpu.make_async_remote_copy(
            src_ref=ref, dst_ref=ref, send_sem=rsem,
            recv_sem=rsem, device_id=target(partner), device_id_type=MESH,
        ).wait_recv
        guarded(when, wait)

    def share(ref, k):
        push(ref.at[branch], ref.at[branch], pair_ssem.at[k], pair_rsem.at[k], partner)

    def push_right(b, z, when=None):
        size = most if even or b == wide else least
        push(
            right_send.at[b, :size], right_all.at[me, :size], right_sems.at[0], right_sems.at[1], (b, z), when
        )

    for k, z in enumerate(order):

        @pl.when(z > dap)
        def _():
            pl.semaphore_wait(ready.at[z - 1], nb)

        pl.when(z > dap)(functools.partial(push_left, z))
        if redo:
            push(left_send.at[end], left_last.at[me], last_sems.at[0], last_sems.at[1], (branch, 0), z == 0)
        for b in range(nb):
            push(flag_all.at[me], flag_all.at[me], flag_sems.at[0], flag_sems.at[1], (b, z))
        for b in range(nb):
            push_right(b, z)
            if b == 0 and k + 1 < len(order):
                pl.when(order[k + 1] < dap)(functools.partial(push_left, order[k + 1]))
    for b in range(nb):
        push_right(b, dap, branch != b)
    push(left_send.at[dap], left_all.at[me], pass_sems.at[0], pass_sems.at[1], partner)
    push(flag_all.at[me], flag_all.at[me], flag_sems.at[0], flag_sems.at[1], partner)
    loaded(3, 4)
    share(class_all, 0)
    share(couple_all, 1)
    left_all[me] = left_send[dap]
    right_all[me, :least] = right_send[branch, :least]
    if not even:

        @pl.when(branch == wide)
        def _():
            right_all[me, least:] = right_send[wide, least:]

    if redo:

        @pl.when(dap == 0)
        def _():
            left_last[me] = left_send[end]

    loaded(8, 9, 10, 11)
    chip_pairs = nb * pairs
    lane_pair = iota((1, chip_pairs), 1)
    key_pair = lane_keys(chip_pairs)
    residue = (lane_pair // pairs * nz + dap) * rows + lax.rem(lane_pair // amino, rows)
    ilane = dot(aflag, (iota((amino, chip_pairs), 0) == residue).astype(BF16))[0:1, :]
    key_pair = jnp.where(ilane > 0.5, key_pair, 0.0).astype(jnp.int32)
    slot = iota((slots, 1), 0)
    gather = jnp.where(
        (key_pair == side * part + slot // block_rows + 1) & (lane_pair // amino == lax.rem(slot, block_rows)),
        1.0,
        0.0,
    ).astype(BF16)
    eye = iota((amino, amino), 0) == iota((amino, amino), 1)
    wide_key = jnp.broadcast_to(lane_keys(amino), (amino, amino))
    key_col = jnp.sum(jnp.where(eye, wide_key, 0.0), axis=1, keepdims=True).astype(jnp.int32)
    key_col = jnp.concatenate([key_col] * rows, axis=0)
    col = iota((1, nb * slots), 1)
    expand = jnp.where(
        (key_col == (nb - 1 - col // slots) * part + lax.rem(col, slots) // block_rows + 1)
        & (iota((pairs, 1), 0) // amino + branch * rows == lax.rem(col, block_rows)),
        1.0,
        0.0,
    ).astype(BF16)
    expand = jnp.concatenate([expand, expand], axis=1)
    arrived(class_all.at[other], pair_rsem.at[0])
    arrived(couple_all.at[other], pair_rsem.at[1])
    bins = embed_ref.shape[0]
    hot = []
    for b in range(nb):
        for i in range(rows):
            column = jnp.sum(
                jnp.where(eye, class_all[b, i : i + 1, :], 0).astype(F32), axis=1, keepdims=True
            ).astype(jnp.int32)
            hot.append(jnp.where(column == iota((amino, bins), 1), 1.0, 0.0))
    onehot = jnp.concatenate(hot, axis=0).astype(BF16)
    couple = couple_all[...].reshape(chip_pairs, width)
    base_buf[...] = (couple.astype(F32) + dot(onehot, embed_ref[...])).reshape(nb, pairs, width)
    base_c = dot(gather, couple) + dot(dot(gather, onehot).astype(BF16), embed_ref[...])

    if redo:

        @pl.when(dap == end)
        def _():
            base_send[...] = base_c.astype(BF16)

        push(base_send, base_last, base_sems.at[0], base_sems.at[1], (branch, 0), dap == end)

    for z in chips:
        d = branch * nz + z
        arrived(left_all.at[d], left_rsem.at[z - (z > dap)])
        push(left_all.at[d], left_all.at[d], pass_sems.at[0], pass_sems.at[1], partner)
    if redo:
        arrived(left_last.at[: nz - 1], last_sems.at[1], dap == 0)
        lasts = left_last.at[pl.ds(branch * nz, nz)]
        push(lasts, lasts, last_sems.at[2], last_sems.at[3], partner, dap == 0)
    if even:
        arrived(right_all.at[: n - 1], right_sems.at[1])
    else:
        arrived(right_all.at[: n - 1], right_sems.at[1], branch == wide)
        arrived(right_all.at[: n - 1, :least], right_sems.at[1], branch != wide)
    arrived(left_all.at[:nz], pass_sems.at[1])
    arrived(flag_all.at[: n - 1], flag_sems.at[1])

    number = jnp.maximum(jnp.sum(flag_all[...], axis=0), 1.0)
    right = jnp.concatenate([right_all[:, t].reshape(n * seqs, LANES) for t in range(groups)], axis=1)
    lane = iota((1, LANES), 1)

    def middle(left_ref, base):
        left = jnp.concatenate([left_ref[:, b].reshape(n * seqs, LANES) for b in range(nb)], axis=1)
        outer = lax.dot_general(left, right, (((0,), (0,)), ((), ())), preferred_element_type=F32)
        for t in range(groups):
            for i in range(block_rows):
                outer_buf[t, pl.ds(i * (inner + 1), inner), :] = outer[
                    i * inner : (i + 1) * inner, t * LANES : (t + 1) * LANES
                ]
        parts = [[] for _ in range(part)]
        for t in range(groups):
            for q in range(inner // reps):
                block = [outer_buf[t, pl.ds(q * reps + g, block_rows, stride=inner + 1), :] for g in range(reps)]
                span = reps // 2
                while span:
                    upper = (lane // (span * inner)) % 2 == 1
                    new = list(block)
                    for a in range(reps):
                        if a & span:
                            continue
                        b = a | span
                        shift = span * inner
                        if 2 * shift == LANES:
                            moved = pltpu.roll(jnp.where(upper, block[a], block[b]), shift, 1)
                            new[a] = jnp.where(upper, moved, block[a])
                            new[b] = jnp.where(upper, block[b], moved)
                        else:
                            new[a] = jnp.where(upper, pltpu.roll(block[b], shift, 1), block[a])
                            new[b] = jnp.where(upper, block[b], pltpu.roll(block[a], LANES - shift, 1))
                    block = new
                    span //= 2
                for g in range(reps):
                    parts[t * reps + g].append(block[g])
        packed = jnp.concatenate([jnp.concatenate(p, axis=1) for p in parts], axis=0).astype(BF16)
        product = dot(packed, tall_ref[:long]) / number
        pair_c = standardize(base + product, gain_ref[0]).astype(BF16)
        right_two = dot(pair_c, wedge_ref[:, 2 * width :])
        tri_right = jax.nn.sigmoid(right_two[:, :width]) * right_two[:, width:]
        return product, pair_c, tri_right.astype(BF16)

    product, pair_c, tri_all[dap] = middle(left_all, base_c)
    full = None if even else branch == wide
    short = None if even else branch != wide

    def tri_block(z, size):
        return tri_all.at[z, :size]

    for z in chips:
        skip = redo & (dap == end) & (z == 0)
        if even:
            push(tri_all.at[dap], tri_all.at[dap], tri_ssem.at[0], tri_rsem.at[rank_at(z)], (branch, z), ~skip)
        else:
            for size, when in ((slots, full), (firm, short)):
                push(
                    tri_block(dap, size), tri_block(dap, size), tri_ssem.at[0], tri_rsem.at[rank_at(z)], (branch, z),
                    when & ~skip,
                )

    product_all[branch] = product
    share(product_all, 2)

    def edges():
        left_two = dot(pair_c, wedge_ref[:, : 2 * width])
        edge_buf[...] = (jax.nn.sigmoid(left_two[:, :width]) * left_two[:, width:]).astype(BF16).astype(F32)
        for i in range(block_rows):
            for k in range(part):
                row = edge_buf[k * block_rows + i : k * block_rows + i + 1, :]
                spread_buf[i, k * SUB : (k + 1) * SUB, :] = jnp.broadcast_to(row, (SUB, width))

    def triangle(z, side, store):
        block = tri_all[z].astype(F32)
        for i in range(rows):
            both = spread_buf[side * rows + i] * block
            store[z, i] = jnp.sum(both.reshape(part, SUB, width), axis=0)

    def contribute(z):
        triangle(z, other, part_send)
        push(part_send.at[z], part_in.at[z], part_ssem.at[0], part_rsem.at[0], partner)
        triangle(z, branch, own_buf)

    def settle(z):
        for i in range(rows):
            total = own_buf[z, i] + part_in[z, i]
            for b in range(nb):
                row = i * amino + (b * nz + z) * rows
                tri_buf[pl.ds(pl.multiple_of(row, rows), rows), :] = total[b * rows : (b + 1) * rows]

    if not redo:
        edges()
        contribute(dap)
    if redo:

        @pl.when(dap == 0)
        def _():
            arrived(left_last.at[:nz], last_sems.at[3])
            arrived(base_last, base_sems.at[1])
            tri_all[end] = middle(left_last, base_last[...].astype(F32))[2]
            edges()

        pl.when(dap != 0)(edges)
        contribute(dap)

        @pl.when(dap == 0)
        def _():
            contribute(end)

    def refresh():
        arrived(product_all.at[other], pair_rsem.at[2])
        whole = product_all[...].reshape(nb * slots, width)
        high = whole.astype(BF16)
        rest = (whole - high.astype(F32)).astype(BF16)
        updated = base_buf[branch] + dot(expand, jnp.concatenate([high, rest], axis=0))
        pair = standardize(updated, gain_ref[0]).astype(BF16)
        updated_buf[...] = updated
        gate_buf[...] = jax.nn.sigmoid(dot(pair, tall_ref[long : long + width]))

    pl.when(dap != 0)(refresh)
    late = [jnp.where(dap == 0, end - k, (k + 1 + (k + 1 >= dap)) % nz) for k in range(nz - 1)]
    late = [jnp.where((dap == 0) | (k < nz - 2), z, 0) for k, z in enumerate(late)]
    for k, z in enumerate(late):
        skip = redo & (dap == 0) & (z == end)

        @pl.when(~skip)
        def _():
            if even:
                arrived(tri_all.at[z], tri_rsem.at[z - (z > dap)])
            else:
                arrived(tri_block(z, slots), tri_rsem.at[z - (z > dap)], full)
                arrived(tri_block(z, firm), tri_rsem.at[z - (z > dap)], short)
            contribute(z)
    pl.when(dap == 0)(refresh)
    arrived(part_in, part_rsem.at[0])
    for z in range(nz):
        settle(z)
    tri = standardize(tri_buf[:pairs], gain_ref[1]).astype(BF16)
    out_ref[...] = (updated_buf[...] + gate_buf[...] * dot(tri, tall_ref[long + width :])).astype(BF16)
    for b in range(nb):
        size = most if even or b == wide else least
        drain(right_all.at[: nz - 1, :size], right_sems.at[0])
        drain(right_all.at[:1, :size], right_sems.at[0], branch != b)
    drain(left_all.at[: n - 1], pass_sems.at[0])
    drain(flag_all.at[: n - 1], flag_sems.at[0])
    if redo:
        drain(left_last.at[0], last_sems.at[0], dap != 0)
        drain(left_last.at[:nz], last_sems.at[2], dap == 0)
        drain(base_send, base_sems.at[0], dap == end)
    for fewer, last in ((1, redo & (dap == end)), (0, ~(redo & (dap == end)))):
        if even:
            drain(tri_all.at[: nz - 1 - fewer], tri_ssem.at[0], last)
        else:
            drain(tri_all.at[: nz - 1 - fewer], tri_ssem.at[0], last & full)
            drain(tri_all.at[: nz - 1 - fewer, :firm], tri_ssem.at[0], last & short)
    drain(part_send, part_ssem.at[0])
    for k, ref in enumerate((class_all, couple_all, product_all)):
        drain(ref.at[branch], pair_ssem.at[k])


def on_device(nb, nz, x, hflags, aflags, classes, couple, hgain, wl, wr, wout, embed, cgain, wedge, wgate, wfin, tgain):
    n = nb * nz
    seqs, amino, depth = x.shape
    rows, _, width = couple.shape
    inner = wl.shape[1]
    live = amino - 3 * amino // 8
    groups = -(-(live // (LANES // inner)) // nb)
    part = groups * (LANES // inner)
    slots = part * nb * rows
    dma = pltpu.SemaphoreType.DMA
    operands = (
        x.reshape(seqs * amino, depth), hflags.reshape(1, seqs), aflags.reshape(1, amino), classes,
        couple.reshape(rows * amino, width), hgain.reshape(1, depth), wl.T, wr.T, wout, embed,
        cgain.reshape(1, width), wedge, wgate, wfin, tgain.reshape(1, width),
    )
    shapes = [a.shape for a in operands]
    shapes[3], shapes[4] = (nb, *shapes[3]), (nb, *shapes[4])
    held = [pltpu.VMEM(shapes[k], operands[k].dtype) for k in range(6)] + [
        pltpu.VMEM((2, inner, depth), BF16),
        pltpu.VMEM((inner * inner + 2 * width, width), BF16),
        pltpu.VMEM(shapes[9], BF16),
        pltpu.VMEM((2, 1, width), F32),
        pltpu.VMEM(shapes[11], BF16),
    ]
    out = pl.pallas_call(
        functools.partial(kernel, nb, nz),
        out_shape=pltpu.VMEM((rows * amino, width), BF16),
        in_specs=[pl.BlockSpec(memory_space=pl.ANY)] * OPERANDS,
        out_specs=pl.BlockSpec(memory_space=pltpu.VMEM),
        scratch_shapes=held
        + [
            dma((HELD,)),
            pltpu.VMEM((n, 1, LANES), F32),
            pltpu.VMEM((nb, groups, seqs, LANES), BF16),
            pltpu.VMEM((n, groups, seqs, LANES), BF16),
            pltpu.VMEM((nz, nb, seqs, LANES), BF16),
            pltpu.VMEM((n, nb, seqs, LANES), BF16),
            pltpu.VMEM((n, nb, seqs, LANES), BF16),
            pltpu.VMEM((nz, slots, width), BF16),
            pltpu.VMEM(((seqs + 1) * (amino + 1), LANES), F32),
            pltpu.VMEM((groups, (nb * rows + 1) * (inner + 1), LANES), F32),
            pltpu.VMEM((nb, rows * amino, width), F32),
            pltpu.VMEM((slots, width), BF16),
            pltpu.VMEM((slots, width), BF16),
            pltpu.VMEM((nb, slots, width), F32),
            pltpu.VMEM((slots, width), F32),
            pltpu.VMEM((nb * rows, slots, width), F32),
            pltpu.VMEM((nz, rows, SUB, width), F32),
            pltpu.VMEM((nz, rows, SUB, width), F32),
            pltpu.VMEM((nz, rows, SUB, width), F32),
            pltpu.VMEM((rows * amino + SUB, width), F32),
            pltpu.VMEM((rows * amino, width), F32),
            pltpu.VMEM((rows * amino, width), F32),
        ]
        + [dma((2,)), dma((2,)), dma((2,)), dma((4,)), dma((2,)), dma((nz - 1,))]
        + [dma((1,)), dma((nz - 1,)), dma((1,)), dma((1,)), dma((3,)), dma((3,))]
        + [pltpu.SemaphoreType.REGULAR((nz - 1,))],
        compiler_params=pltpu.CompilerParams(collective_id=0, has_side_effects=True),
    )(*operands)
    return out.reshape(rows, amino, width)


def solution(mesh):
    split = ("rep", "branch", "dap")
    placed = (
        P(split, None, None), P(split), P("rep"), P(split, None), P(split, None, None),
        P(), P(), P(), P(), P(), P(), P(), P(), P(), P(),
    )
    return jax.shard_map(
        functools.partial(on_device, mesh.shape["branch"], mesh.shape["dap"]),
        mesh=mesh,
        in_specs=placed,
        out_specs=P(split, None, None),
        check_vma=False,
    )
```
